512 devices in a mesh: row: 16 (over x, y_lo), col: 32 (over y_hi, z, core).
Axes of the slice: x: 4, y: 8 (y_hi: 2, y_lo: 4; y = y_hi * 4 + y_lo), z: 8, core: 2. Of those that a mesh axis runs over, the one named last changes fastest.
Arguments:
- source_map: float32 [8192, 8192], P('row', 'col'), may hold values from -6 to 6
- observed: float32 [8192, 8192], P('row', 'col'), may hold values from -6 to 6
- factor_x: float32 [32, 3, 256, 256], P('row'), may hold values from -0.21875 to 0.21875
- band_x: int32 [32, 3], P('row'), may hold values 0 or 1
- factor_y: float32 [32, 3, 256, 256], P('col'), may hold values from -0.21875 to 0.21875
- band_y: int32 [32, 3], P('col'), may hold values 0 or 1
- step_size: float32 [1], replicated, may hold values from 0.03 to 0.08
- threshold: float32 [1], replicated, may hold values from 0.1 to 0.4
Outputs:
- estimate: float32 [8192, 8192], P('row', 'col')
The draws below stay inside these ranges and needn't reach their ends.
All inputs are finite; a program needn't handle non-finite values. No bound on the sum of `band_x` or of `band_y` on one device may be relied on, other than what follows from the above.
Results may differ from the reference program's by a relative error of at most 0.0003.
Values sent between devices are 32-bit elements; how exact they have to be, the bound alone decides.
No kernel may reach another device: no remote copies, remote signals or barrier semaphores. Data moves between devices by JAX's collectives and lax.ppermute only.
A program may use at most 64 MiB of HBM per device.

```python
import jax
import jax.numpy as jnp
from jax import lax

N = 8192
BLK = 256
ITERS = 2
NB = 32


def place_ends(entries, stream_key, least, top_value):
    index_at = [jax.random.randint(jax.random.fold_in(stream_key, axis), (), 0, length) for axis, length in enumerate(entries.shape)]
    widest = entries.shape.index(max(entries.shape))
    neighbour = index_at[:widest] + [(index_at[widest] + 1) % entries.shape[widest]] + index_at[widest + 1:]
    return entries.at[tuple(index_at)].set(least).at[tuple(neighbour)].set(top_value)


def levels(rng, dims, shards, least, top_value):
    def one(dim, blocks):
        draws = jax.random.uniform(jax.random.fold_in(jax.random.fold_in(rng, 6), dim), (blocks,), jnp.float32, least / len(shards), top_value / len(shards))
        return jnp.repeat(jnp.exp(draws), dims[dim] // blocks).reshape((-1,) + (1,) * (len(dims) - dim - 1))

    loudness = one(*shards[0])
    for cut in shards[1:]:
        loudness = loudness * one(*cut)
    return loudness


def centred(rng, shape, width, bound, pieces=(), dtype=jnp.bfloat16):
    level = levels(rng, shape, pieces, -0.22, 0.18) if pieces else 1.0
    array = jax.random.normal(rng, shape, jnp.float32) * width * level
    return jnp.minimum(jnp.maximum(array, -bound), bound).astype(dtype)


def setup_inputs(seed: int = 0) -> dict:
    key_of = jax.random.split(jax.random.key(seed), 9)
    return {
        "source_map": centred(key_of[0], (N, N), 1.0, 6.0, ((0, 16), (1, 32)), jnp.float32),
        "observed": centred(key_of[1], (N, N), 1.0, 6.0, ((0, 16), (1, 32)), jnp.float32),
        "factor_x": centred(key_of[2], (NB, 3, BLK, BLK), (3 * BLK) ** -0.5, 0.21875, ((0, 16),), jnp.float32),
        "band_x": place_ends((jax.random.randint(key_of[3], (NB, 3), 0, 3) < 2).astype(jnp.int32), jax.random.fold_in(key_of[3], 1), 0, 1),
        "factor_y": centred(key_of[4], (NB, 3, BLK, BLK), (3 * BLK) ** -0.5, 0.21875, ((0, 32),), jnp.float32),
        "band_y": place_ends((jax.random.randint(key_of[5], (NB, 3), 0, 3) < 2).astype(jnp.int32), jax.random.fold_in(key_of[5], 1), 0, 1),
        "step_size": jnp.clip(jax.random.uniform(key_of[6], (1,), jnp.float32, 0.03, 0.08), 0.03, 0.08),
        "threshold": jnp.clip(jax.random.uniform(key_of[7], (1,), jnp.float32, 0.1, 0.4), 0.1, 0.4),
    }


highest = lax.Precision.HIGHEST


def shrink(values, amount):
    return jnp.sign(values) * jnp.maximum(jnp.abs(values) - amount, 0.0)


def reference(source_map, observed, factor_x, band_x, factor_y, band_y, step_size, threshold):
    block_count = N // BLK
    masked_x = factor_x * band_x.astype(jnp.float32)[:, :, None, None]
    masked_y = factor_y * band_y.astype(jnp.float32)[:, :, None, None]
    padded_fx = jnp.pad(masked_x, ((1, 1), (0, 0), (0, 0), (0, 0)))
    padded_fy = jnp.pad(masked_y, ((1, 1), (0, 0), (0, 0), (0, 0)))
    current = source_map
    for iteration in range(ITERS):
        blocks = jnp.pad(current.reshape(block_count, BLK, N), ((1, 1), (0, 0), (0, 0)))
        left_product = jnp.zeros((block_count, BLK, N), jnp.float32)
        for slot_index in range(3):
            left_product = left_product + jnp.einsum("rij,rjn->rin", masked_x[:, slot_index], blocks[slot_index:slot_index + block_count], precision=highest)
        padded_left = jnp.pad(left_product.reshape(N, block_count, BLK), ((0, 0), (1, 1), (0, 0)))
        forward = jnp.zeros((N, block_count, BLK), jnp.float32)
        for slot_index in range(3):
            forward = forward + jnp.einsum("njb,jab->nja", padded_left[:, slot_index:slot_index + block_count], masked_y[:, slot_index], precision=highest)
        misfit = forward.reshape(N, N) - observed
        misfit_blocks = jnp.pad(misfit.reshape(block_count, BLK, N), ((1, 1), (0, 0), (0, 0)))
        adjoint_rows = jnp.zeros((block_count, BLK, N), jnp.float32)
        for slot_index in range(3):
            first = 2 - slot_index
            adjoint_rows = adjoint_rows + jnp.einsum("cij,cin->cjn", padded_fx[first:first + block_count, slot_index], misfit_blocks[first:first + block_count], precision=highest)
        padded_adjoint = jnp.pad(adjoint_rows.reshape(N, block_count, BLK), ((0, 0), (1, 1), (0, 0)))
        gradient = jnp.zeros((N, block_count, BLK), jnp.float32)
        for slot_index in range(3):
            first = 2 - slot_index
            gradient = gradient + jnp.einsum("nca,cab->ncb", padded_adjoint[:, first:first + block_count], padded_fy[first:first + block_count, slot_index], precision=highest)
        current = shrink(current - step_size[0] * gradient.reshape(N, N), threshold[0])
    return current
```

```python
import jax
import jax.numpy as jnp
from jax import lax
from jax.experimental import pallas as pl
from jax.experimental.pallas import tpu as pltpu
from jax.sharding import PartitionSpec as P

f32 = jnp.float32
bf16 = jnp.bfloat16
VMEM = pl.BlockSpec(memory_space=pltpu.VMEM)
SMEM = pl.BlockSpec(memory_space=pltpu.SMEM)


def split(x):
    hi = x.astype(bf16)
    return hi, (x - hi.astype(f32)).astype(bf16)


def dot3(xh, xl, yh, yl):
    mm = lambda a, b: jnp.dot(a, b, preferred_element_type=f32)
    return mm(xh, yh) + (mm(xh, yl) + mm(xl, yh))


def soft(v, h):
    return v - jnp.minimum(jnp.maximum(v, -h), h)


def call(body, ins, outs, flops, scratch=(), limit=24 << 20):
    size = lambda a: a.size * a.dtype.itemsize
    return pl.pallas_call(
        body,
        out_shape=[jax.ShapeDtypeStruct(s, d) for s, d in outs],
        in_specs=[SMEM if a.size < 64 else VMEM for a in ins],
        out_specs=[VMEM for _ in outs],
        scratch_shapes=list(scratch),
        compiler_params=pltpu.CompilerParams(vmem_limit_bytes=limit),
        cost_estimate=pl.CostEstimate(
            flops=flops, bytes_accessed=sum(size(a) for a in ins), transcendentals=0
        ),
    )(*ins)


def prepare(fx, bx, fy, by, pos):
    blk = fx.shape[2]

    def body(fx, bx, fy, by, pos, axh, axl, atxh, atxl, byh, byl, byth, bytl):
        row, rows, col, cols = pos[0], pos[1], pos[2], pos[3]

        def put(v, k, plain, trans):
            s = slice(k * blk, (k + 1) * blk)
            plain[0][:, s], plain[1][:, s] = split(v)
            trans[0][s, :], trans[1][s, :] = split(v.T)

        for r in range(2):
            for s in range(3):
                m = bx[r, s].astype(f32)
                if (r, s) == (0, 0):
                    m = jnp.where(row == 0, 0.0, m)
                if (r, s) == (1, 2):
                    m = jnp.where(row == rows - 1, 0.0, m)
                put(fx[r, s] * m, s, (axh.at[r], axl.at[r]), (atxh.at[r], atxl.at[r]))
        first = jnp.where(col % 2 == 0, 2, 0)
        for k, s in enumerate((first, 1, 2 - first)):
            m = by[0, s].astype(f32)
            m = jnp.where((s == 0) & (col == 0), 0.0, m)
            m = jnp.where((s == 2) & (col == cols - 1), 0.0, m)
            put(fy[0, s] * m, k, (byh, byl), (byth, bytl))

    outs = [((2, blk, 3 * blk), bf16)] * 2 + [((2, 3 * blk, blk), bf16)] * 2
    outs += [((blk, 3 * blk), bf16)] * 2 + [((3 * blk, blk), bf16)] * 2
    o = call(body, (fx, bx, fy, by, pos), outs, 1 << 24)
    return o[0:2], o[2:4], o[4:6], o[6:8]


def left(ax, xs, u):
    blk = xs[0].shape[0] // 4
    for r in range(2):
        s = slice(r * blk, (r + 3) * blk)
        u[r * blk : (r + 1) * blk, :] = dot3(ax[0][r], ax[1][r], xs[0][s, :], xs[1][s, :])


def apply_left(x, up, down, ax):
    blk, n = up.shape

    def body(x, up, down, axh, axl, u, xh, xl):
        for t, v in enumerate((up[...], x[:blk, :], x[blk:, :], down[...])):
            s = slice(t * blk, (t + 1) * blk)
            xh[s, :], xl[s, :] = split(v)
        left((axh, axl), (xh, xl), u)

    scratch = [pltpu.VMEM((4 * blk, n), bf16)] * 2
    return call(body, (x, up, down, *ax), [(x.shape, f32)], 36 * blk * blk * n, scratch)[0]


def right(ua, u, ub, observed, byt, by):
    m, blk = u.shape
    chunk = 256

    def body(ua, u, ub, obs, byth, bytl, byh, byl, qa, q, qb):
        for i in range(m // chunk):
            r = slice(i * chunk, (i + 1) * chunk)
            acc = -obs[r, :]
            for k, v in enumerate((ua, u, ub)):
                s = slice(k * blk, (k + 1) * blk)
                vh, vl = split(v[r, :])
                acc = acc + dot3(vh, vl, byth[s, :], bytl[s, :])
            mh, ml = split(acc)
            for k, o in enumerate((qa, q, qb)):
                s = slice(k * blk, (k + 1) * blk)
                o[r, :] = dot3(mh, ml, byh[:, s], byl[:, s])

    return call(body, (ua, u, ub, observed, *byt, *by), [(u.shape, f32)] * 3, 72 * m * blk * blk)


def back_left(q, ra, rb, atx, merged):
    m, n = q.shape
    blk = m // 2

    def body(q, ra, rb, ah, al, *outs):
        p = []
        for r in range(2):
            s = slice(r * blk, (r + 1) * blk)
            vh, vl = split(q[s, :] + ra[s, :] + rb[s, :])
            p.append(dot3(ah[r], al[r], vh, vl))
        p0 = p[0][:blk]
        p1 = p[0][blk : 2 * blk] + p[1][:blk]
        p2 = p[0][2 * blk :] + p[1][blk : 2 * blk]
        p3 = p[1][2 * blk :]
        if merged:
            top, bottom = outs
            top[:blk, :], top[blk:, :] = p0, p1
            bottom[:blk, :], bottom[blk:, :] = p2, p3
        else:
            top, mid, bottom = outs
            top[...], bottom[...] = p0, p3
            mid[:blk, :], mid[blk:, :] = p1, p2

    outs = [((m, n), f32)] * 2 if merged else [((blk, n), f32), ((m, n), f32), ((blk, n), f32)]
    return call(body, (q, ra, rb, *atx), outs, 36 * blk * blk * n)


def update_left(top, bottom, rtop, rbottom, x, up, down, sc, ax):
    blk, n = up.shape

    def body(top, bottom, rtop, rbottom, x, up, down, sc, axh, axl, xn, u, xh, xl):
        step, h = sc[0], sc[1]
        lo, hi = slice(0, blk), slice(blk, 2 * blk)
        parts = ((up[...], top, rtop, lo), (x[lo, :], top, rtop, hi))
        parts += ((x[hi, :], bottom, rbottom, lo), (down[...], bottom, rbottom, hi))
        for t, (v, a, b, s) in enumerate(parts):
            new = soft(v - step * (a[s, :] + b[s, :]), h)
            if t in (1, 2):
                xn[(t - 1) * blk : t * blk, :] = new
            d = slice(t * blk, (t + 1) * blk)
            xh[d, :], xl[d, :] = split(new)
        left((axh, axl), (xh, xl), u)

    scratch = [pltpu.VMEM((4 * blk, n), bf16)] * 2
    ins = (top, bottom, rtop, rbottom, x, up, down, sc, *ax)
    return call(body, ins, [(x.shape, f32)] * 2, 36 * blk * blk * n, scratch)


def update(mid, rup, rdown, x, sc):
    blk, n = rup.shape

    def body(mid, rup, rdown, x, sc, o):
        step, h = sc[0], sc[1]
        lo, hi = slice(0, blk), slice(blk, 2 * blk)
        for s, r in ((lo, rup), (hi, rdown)):
            o[s, :] = soft(x[s, :] - step * (mid[s, :] + r[...]), h)

    return call(body, (mid, rup, rdown, x, sc), [(x.shape, f32)], 1 << 20)[0]


def per_device(x, observed, fx, bx, fy, by, step_size, threshold):
    blk = fx.shape[2]
    rows, cols = lax.axis_size("row"), lax.axis_size("col")
    downward = [(i, i + 1) for i in range(rows - 1)]
    upward = [(i + 1, i) for i in range(rows - 1)]
    pairs = []
    for first in (0, 1):
        forth = [(i, i + 1) for i in range(first, cols - 1, 2)]
        pairs.append(forth + [(j, i) for i, j in forth])

    def row_swap(to_up, to_down):
        from_up = lax.ppermute(to_down, "row", downward)
        from_down = lax.ppermute(to_up, "row", upward)
        return from_up, from_down

    def col_swap(a, b):
        rb = lax.ppermute(b, "col", pairs[1])
        ra = lax.ppermute(a, "col", pairs[0])
        return ra, rb

    pos = jnp.stack([lax.axis_index("row"), rows, lax.axis_index("col"), cols]).astype(jnp.int32)
    sc = jnp.concatenate([step_size, threshold])
    up, down = row_swap(x[:blk], x[blk:])
    ax, atx, byf, byt = prepare(fx, bx, fy, by, pos)
    u = apply_left(x, up, down, ax)
    ua, ub = col_swap(u, u)
    qa, q, qb = right(ua, u, ub, observed, byt, byf)
    ra, rb = col_swap(qa, qb)
    top, bottom = back_left(q, ra, rb, atx, True)
    rtop, rbottom = row_swap(top, bottom)
    x, u = update_left(top, bottom, rtop, rbottom, x, up, down, sc, ax)
    ua, ub = col_swap(u, u)
    qa, q, qb = right(ua, u, ub, observed, byt, byf)
    ra, rb = col_swap(qa, qb)
    top, mid, bottom = back_left(q, ra, rb, atx, False)
    rup, rdown = row_swap(top, bottom)
    return update(mid, rup, rdown, x, sc)


def solution(mesh):
    in_specs = (
        P("row", "col"),
        P("row", "col"),
        P("row", None, None, None),
        P("row", None),
        P("col", None, None, None),
        P("col", None),
        P(),
        P(),
    )
    return jax.shard_map(
        per_device, mesh=mesh, in_specs=in_specs, out_specs=P("row", "col"), check_vma=False
    )
```

```python
import jax
import jax.numpy as jnp
from jax import lax
from jax.experimental import pallas as pl
from jax.experimental.pallas import tpu as pltpu
from jax.sharding import PartitionSpec as P

f32 = jnp.float32
bf16 = jnp.bfloat16
VMEM = pl.BlockSpec(memory_space=pltpu.VMEM)
SMEM = pl.BlockSpec(memory_space=pltpu.SMEM)
CHUNK = 256


def split(x):
    hi = x.astype(bf16)
    return hi, (x - hi.astype(f32)).astype(bf16)


def dot3(xh, xl, yh, yl):
    mm = lambda a, b: jnp.dot(a, b, preferred_element_type=f32)
    return mm(xh, yh) + (mm(xh, yl) + mm(xl, yh))


def soft(v, h):
    return v - jnp.minimum(jnp.maximum(v, -h), h)


def call(body, ins, outs, flops, scratch=(), limit=24 << 20):
    size = lambda a: a.size * a.dtype.itemsize
    return pl.pallas_call(
        body,
        out_shape=[jax.ShapeDtypeStruct(s, d) for s, d in outs],
        in_specs=[SMEM if a.size < 64 else VMEM for a in ins],
        out_specs=[VMEM for _ in outs],
        scratch_shapes=list(scratch),
        compiler_params=pltpu.CompilerParams(vmem_limit_bytes=limit),
        cost_estimate=pl.CostEstimate(
            flops=flops, bytes_accessed=sum(size(a) for a in ins), transcendentals=0
        ),
    )(*ins)


def prepare(fx, bx, fy, by, pos):
    blk = fx.shape[2]

    def body(fx, bx, fy, by, pos, axh, axl, atxh, atxl, byh, byl, byth, bytl, fb):
        row, rows, col, cols = pos[0], pos[1], pos[2], pos[3]

        def put(v, k, plain, trans):
            s = slice(k * blk, (k + 1) * blk)
            plain[0][:, s], plain[1][:, s] = split(v)
            trans[0][s, :], trans[1][s, :] = split(v.T)

        for r in range(2):
            for s in range(3):
                m = bx[r, s].astype(f32)
                if (r, s) == (0, 0):
                    m = jnp.where(row == 0, 0.0, m)
                if (r, s) == (1, 2):
                    m = jnp.where(row == rows - 1, 0.0, m)
                put(fx[r, s] * m, s, (axh.at[r], axl.at[r]), (atxh.at[r], atxl.at[r]))
        first = jnp.where(col % 2 == 0, 2, 0)
        for k, s in enumerate((first, 1, 2 - first)):
            m = by[0, s].astype(f32)
            m = jnp.where((s == 0) & (col == 0), 0.0, m)
            m = jnp.where((s == 2) & (col == cols - 1), 0.0, m)
            v = fy[0, s] * m
            put(v, k, (byh, byl), (byth, bytl))
        fb[...] = v

    outs = [((2, blk, 3 * blk), bf16)] * 2 + [((2, 3 * blk, blk), bf16)] * 2
    outs += [((blk, 3 * blk), bf16)] * 2 + [((3 * blk, blk), bf16)] * 2
    outs += [((blk, blk), f32)]
    o = call(body, (fx, bx, fy, by, pos), outs, 1 << 24)
    return o[0:2], o[2:4], o[4:6], o[6:8], o[8]


def left(ax, xs, u):
    blk = xs[0].shape[0] // 4
    for r in range(2):
        s = slice(r * blk, (r + 3) * blk)
        u[r * blk : (r + 1) * blk, :] = dot3(ax[0][r], ax[1][r], xs[0][s, :], xs[1][s, :])


def apply_left(x, up, down, ax):
    blk, n = up.shape

    def body(x, up, down, axh, axl, u, xh, xl):
        for t, v in enumerate((up[...], x[:blk, :], x[blk:, :], down[...])):
            s = slice(t * blk, (t + 1) * blk)
            xh[s, :], xl[s, :] = split(v)
        left((axh, axl), (xh, xl), u)

    scratch = [pltpu.VMEM((4 * blk, n), bf16)] * 2
    return call(body, (x, up, down, *ax), [(x.shape, f32)], 36 * blk * blk * n, scratch)[0]


def near_misfit(u, ua, observed, byt, *below):
    m, blk = u.shape

    def body(u, ua, obs, byth, bytl, *rest):
        w = rest[-1]
        for v in rest[:-1]:
            w[m:, :] = v[...]
        for i in range(0, m, CHUNK):
            r = slice(i, i + CHUNK)
            acc = -obs[r, :]
            for k, v in enumerate((ua, u)):
                s = slice(k * blk, (k + 1) * blk)
                acc = acc + dot3(*split(v[r, :]), byth[s, :], bytl[s, :])
            w[r, :] = acc

    out = (m + sum(v.shape[0] for v in below), blk)
    return call(body, (u, ua, observed, *byt, *below), [(out, f32)], 24 * m * blk * blk)[0]


def full_misfit(w, ub, byt, by):
    m, blk = ub.shape

    def body(w, ub, byth, bytl, byh, byl, qa, q):
        b = slice(2 * blk, 3 * blk)
        for i in range(0, m, CHUNK):
            r = slice(i, i + CHUNK)
            acc = w[r, :] + dot3(*split(ub[r, :]), byth[b, :], bytl[b, :])
            mh, ml = split(acc)
            for k, o in enumerate((qa, q)):
                s = slice(k * blk, (k + 1) * blk)
                o[r, :] = dot3(mh, ml, byh[:, s], byl[:, s])

    return call(body, (w, ub, *byt, *by), [(ub.shape, f32)] * 2, 36 * m * blk * blk)


def back(q, ra, wb, u, fb, atx, merged):
    m, n = q.shape
    blk = m // 2

    def body(q, ra, wb, u, fb, ah, al, *outs):
        g = fb[fb.shape[0] - blk :, :]
        gh, gl = split(g)
        th, tl = split(g.T)
        p = []
        for r in range(2):
            s = slice(r * blk, (r + 1) * blk)
            other = wb[s, :] + dot3(*split(u[s, :]), th, tl)
            v = q[s, :] + ra[s, :] + dot3(*split(other), gh, gl)
            p.append(dot3(ah[r], al[r], *split(v)))
        p0 = p[0][:blk]
        p1 = p[0][blk : 2 * blk] + p[1][:blk]
        p2 = p[0][2 * blk :] + p[1][blk : 2 * blk]
        p3 = p[1][2 * blk :]
        if merged:
            top, bottom = outs
            top[:blk, :], top[blk:, :] = p0, p1
            bottom[:blk, :], bottom[blk:, :] = p2, p3
        else:
            top, mid, bottom = outs
            top[...], bottom[...] = p0, p3
            mid[:blk, :], mid[blk:, :] = p1, p2

    outs = [((m, n), f32)] * 2 if merged else [((blk, n), f32), ((m, n), f32), ((blk, n), f32)]
    return call(body, (q, ra, wb, u, fb, *atx), outs, 60 * blk * blk * n)


def update_left(top, bottom, rtop, rbottom, x, up, down, sc, ax):
    blk, n = up.shape

    def body(top, bottom, rtop, rbottom, x, up, down, sc, axh, axl, xn, u, xh, xl):
        step, h = sc[0], sc[1]
        lo, hi = slice(0, blk), slice(blk, 2 * blk)
        parts = ((up[...], top, rtop, lo), (x[lo, :], top, rtop, hi))
        parts += ((x[hi, :], bottom, rbottom, lo), (down[...], bottom, rbottom, hi))
        for t, (v, a, b, s) in enumerate(parts):
            new = soft(v - step * (a[s, :] + b[s, :]), h)
            if t in (1, 2):
                xn[(t - 1) * blk : t * blk, :] = new
            d = slice(t * blk, (t + 1) * blk)
            xh[d, :], xl[d, :] = split(new)
        left((axh, axl), (xh, xl), u)

    scratch = [pltpu.VMEM((4 * blk, n), bf16)] * 2
    ins = (top, bottom, rtop, rbottom, x, up, down, sc, *ax)
    return call(body, ins, [(x.shape, f32)] * 2, 36 * blk * blk * n, scratch)


def update(mid, rup, rdown, x, sc):
    blk, n = rup.shape

    def body(mid, rup, rdown, x, sc, o):
        step, h = sc[0], sc[1]
        lo, hi = slice(0, blk), slice(blk, 2 * blk)
        for s, r in ((lo, rup), (hi, rdown)):
            o[s, :] = soft(x[s, :] - step * (mid[s, :] + r[...]), h)

    return call(body, (mid, rup, rdown, x, sc), [(x.shape, f32)], 1 << 20)[0]


def per_device(x, observed, fx, bx, fy, by, step_size, threshold):
    blk = fx.shape[2]
    rows, cols = lax.axis_size("row"), lax.axis_size("col")
    downward = [(i, i + 1) for i in range(rows - 1)]
    upward = [(i + 1, i) for i in range(rows - 1)]
    pairs = []
    for first in (0, 1):
        forth = [(i, i + 1) for i in range(first, cols - 1, 2)]
        pairs.append(forth + [(j, i) for i, j in forth])

    def row_swap(to_up, to_down):
        from_up = lax.ppermute(to_down, "row", downward)
        from_down = lax.ppermute(to_up, "row", upward)
        return from_up, from_down

    def chip_swap(a):
        return lax.ppermute(a, "col", pairs[0])

    def col_swap(b):
        return lax.ppermute(b, "col", pairs[1])

    def columns(u, fb, merged):
        ua = chip_swap(u)
        ub = col_swap(u)
        w = near_misfit(u, ua, observed, byt, fb if merged else jnp.zeros((8, fb.shape[1]), f32))
        wb = col_swap(w)
        qa, q = full_misfit(w, ub, byt, byf)
        ra = chip_swap(qa)
        fb = wb if merged else fb
        return (*back(q, ra, wb, u, fb, atx, merged), fb)

    pos = jnp.stack([lax.axis_index("row"), rows, lax.axis_index("col"), cols]).astype(jnp.int32)
    sc = jnp.concatenate([step_size, threshold])
    up, down = row_swap(x[:blk], x[blk:])
    ax, atx, byf, byt, fb = prepare(fx, bx, fy, by, pos)
    u = apply_left(x, up, down, ax)
    top, bottom, fb = columns(u, fb, True)
    rtop, rbottom = row_swap(top, bottom)
    x, u = update_left(top, bottom, rtop, rbottom, x, up, down, sc, ax)
    top, mid, bottom, _ = columns(u, fb, False)
    rup, rdown = row_swap(top, bottom)
    return update(mid, rup, rdown, x, sc)


def solution(mesh):
    in_specs = (
        P("row", "col"),
        P("row", "col"),
        P("row", None, None, None),
        P("row", None),
        P("col", None, None, None),
        P("col", None),
        P(),
        P(),
    )
    return jax.shard_map(
        per_device, mesh=mesh, in_specs=in_specs, out_specs=P("row", "col"), check_vma=False
    )
```

```python
import jax
import jax.numpy as jnp
from jax import lax
from jax.experimental import pallas as pl
from jax.experimental.pallas import tpu as pltpu
from jax.sharding import PartitionSpec as P


f32 = jnp.float32
bf16 = jnp.bfloat16
VMEM = pl.BlockSpec(memory_space=pltpu.VMEM)
SMEM = pl.BlockSpec(memory_space=pltpu.SMEM)


def split(x):
    hi = x.astype(bf16)
    return hi, (x - hi.astype(f32)).astype(bf16)


def dot3(x, y):
    (xh, xl), (yh, yl) = x, y
    mm = lambda a, b: jnp.dot(a, b, preferred_element_type=f32)
    return mm(xh, yh) + (mm(xh, yl) + mm(xl, yh))


def soft(v, h):
    return v - jnp.minimum(jnp.maximum(v, -h), h)


def call(body, ins, outs, flops, scratch=(), limit=24 << 20):
    size = lambda a: a.size * a.dtype.itemsize
    return pl.pallas_call(
        body,
        out_shape=[jax.ShapeDtypeStruct(s, d) for s, d in outs],
        in_specs=[SMEM if a.size < 64 else VMEM for a in ins],
        out_specs=[VMEM for _ in outs],
        scratch_shapes=list(scratch),
        compiler_params=pltpu.CompilerParams(vmem_limit_bytes=limit),
        cost_estimate=pl.CostEstimate(
            flops=flops, bytes_accessed=sum(size(a) for a in ins), transcendentals=0
        ),
    )(*ins)


def own_is_e(pos):
    return (pos[2] // 2 + pos[2] % 2) % 2 == 1


def prepare(fx, bx, fy, by, pos):
    blk = fx.shape[2]

    def body(fx, bx, fy, by, pos, ah, al, th, tl, fo, outer):
        row, rows, col, cols = pos[0], pos[1], pos[2], pos[3]
        core = col % 2
        for k, s in enumerate((1, 2 - 2 * core, 2 * core)):
            r = slice(k * blk, (k + 1) * blk)
            mx = bx[core, s].astype(f32)
            my = by[0, s].astype(f32)
            if k == 2:
                last = jnp.where(core == 0, 0, rows - 1)
                mx = jnp.where(row == last, 0.0, mx)
                last = jnp.where(core == 0, 0, cols - 1)
                my = jnp.where(col == last, 0.0, my)
            v = fx[core, s] * mx
            ah[:, r], al[:, r] = split(v)
            th[r, :], tl[r, :] = split(v.T)
            w = fy[0, s] * my
            fo[r, :] = w
        outer[:blk, :] = w
        outer[blk:, :] = jnp.zeros((outer.shape[0] - blk, blk), f32)

    outs = [((blk, 3 * blk), bf16)] * 2 + [((3 * blk, blk), bf16)] * 2
    outs += [((3 * blk, blk), f32), ((2 * blk + 8, blk), f32)]
    o = call(body, (fx, bx, fy, by, pos), outs, 1 << 24)
    return o[0:2], o[2:4], o[4], o[5]


def prepare_columns(own, other, pos):
    blk = own.shape[1]

    def body(own, other, pos, wh, wl, nh, nl, eh, el, oh, ol):
        flag = own_is_e(pos)
        e = lambda k: jnp.where(flag, own[k * blk : (k + 1) * blk, :], other[k * blk : (k + 1) * blk, :])
        o = lambda k: jnp.where(flag, other[k * blk : (k + 1) * blk, :], own[k * blk : (k + 1) * blk, :])
        a, b = slice(0, blk), slice(blk, 2 * blk)
        for v, i, j in ((e(0), a, a), (e(1), a, b), (o(0), b, b), (o(1), b, a)):
            nh[i, j], nl[i, j] = split(v)
            wh[j, i], wl[j, i] = split(v.T)
        eh[...], el[...] = split(e(2).T)
        oh[...], ol[...] = split(o(2).T)

    outs = [((2 * blk, 2 * blk), bf16)] * 4 + [((blk, blk), bf16)] * 4
    o = call(body, (own, other, pos), outs, 1 << 24)
    return o[0:2], o[2:4], o[4:6], o[6:8]


def messages(xh, xl, ah, al, wh, wl, obs, e, o):
    blk = ah.shape[0]
    u = dot3((ah[...], al[...]), (xh[...], xl[...]))
    w = dot3(split(u), (wh[...], wl[...])) - obs
    for out, s in ((e, slice(0, blk)), (o, slice(blk, 2 * blk))):
        out[:blk, :] = u[:, s]
        out[blk:, :] = w[:, s]


def first_messages(x, xp, bown, bother, obs, obsp, ax, fw, pos):
    m, blk = x.shape

    def body(x, xp, bown, bother, obs, obsp, ah, al, wh, wl, pos, e, o, x0, ob, xh, xl):
        flag = own_is_e(pos)
        core = pos[2] % 2
        here = pl.ds(pl.multiple_of(core * blk, blk), blk)
        there = pl.ds(pl.multiple_of(blk - core * blk, blk), blk)
        rows = ((x[here, :], xp[here, :]), (x[there, :], xp[there, :]), (bown[...], bother[...]))
        a, b = slice(0, blk), slice(blk, 2 * blk)
        for k, (p, q) in enumerate(rows):
            r = slice(k * blk, (k + 1) * blk)
            ve, vo = jnp.where(flag, p, q), jnp.where(flag, q, p)
            if k == 0:
                x0[:, a], x0[:, b] = ve, vo
            xh[r, a], xl[r, a] = split(ve)
            xh[r, b], xl[r, b] = split(vo)
        p, q = obs[here, :], obsp[...]
        ob[:, a], ob[:, b] = jnp.where(flag, p, q), jnp.where(flag, q, p)
        messages(xh, xl, ah, al, wh, wl, ob[...], e, o)

    outs = [((2 * blk, blk), f32)] * 2 + [((blk, 2 * blk), f32)] * 2
    scratch = [pltpu.VMEM((3 * blk, 2 * blk), bf16)] * 2
    ins = (x, xp, bown, bother, obs, obsp, *ax, *fw, pos)
    return call(body, ins, outs, 60 * blk**3, scratch)


def later_messages(x, xa, xb, obs, ax, fw):
    blk = x.shape[0]

    def body(x, xa, xb, obs, ah, al, wh, wl, e, o, xh, xl):
        for k, v in enumerate((x, xa, xb)):
            r = slice(k * blk, (k + 1) * blk)
            xh[r, :], xl[r, :] = split(v[...])
        messages(xh, xl, ah, al, wh, wl, obs[...], e, o)

    scratch = [pltpu.VMEM((3 * blk, 2 * blk), bf16)] * 2
    return call(body, (x, xa, xb, obs, *ax, *fw), [((2 * blk, blk), f32)] * 2, 60 * blk**3, scratch)


def back(e, o, re, ro, gown, gother, fe, fo, fn, atx, pos):
    blk = e.shape[1]

    def body(e, o, re, ro, gown, gother, eh, el, oh, ol, nh, nl, th, tl, pos, ps, pa, pb, mh, ml):
        flag = own_is_e(pos)
        gp, gq = gown[:blk, :], gother[...]
        outer = []
        sides = (
            (e, re, (eh, el), jnp.where(flag, gp, gq), slice(0, blk)),
            (o, ro, (oh, ol), jnp.where(flag, gq, gp), slice(blk, 2 * blk)),
        )
        for own, got, (fh, fl), g, s in sides:
            m = own[blk:, :] + dot3(split(got[:blk, :]), (fh[...], fl[...]))
            mh[:, s], ml[:, s] = split(m)
            beyond = got[blk:, :] + dot3(split(own[:blk, :]), split(g.T))
            outer.append(dot3(split(beyond), split(g)))
        n = dot3((mh[...], ml[...]), (nh[...], nl[...])) + jnp.concatenate(outer, axis=1)
        nsplit = split(n)
        for k, out in enumerate((ps, pa, pb)):
            r = slice(k * blk, (k + 1) * blk)
            out[...] = dot3((th[r, :], tl[r, :]), nsplit)

    scratch = [pltpu.VMEM((blk, 2 * blk), bf16)] * 2
    ins = (e, o, re, ro, gown, gother, *fe, *fo, *fn, *atx, pos)
    return call(body, ins, [((blk, 2 * blk), f32)] * 3, 96 * blk**3, scratch)


def update(x, ps, ra, rb, sc):
    def body(x, ps, ra, rb, sc, o):
        o[...] = soft(x[...] - sc[0] * (ps[...] + (ra[...] + rb[...])), sc[1])

    return call(body, (x, ps, ra, rb, sc), [(x.shape, f32)], 1 << 20)[0]


def last_update(x, ps, ra, rb, sc, pos):
    blk = x.shape[0]

    def body(x, ps, ra, rb, sc, pos, keep, give):
        flag = own_is_e(pos)
        v = soft(x[...] - sc[0] * (ps[...] + (ra[...] + rb[...])), sc[1])
        keep[...] = jnp.where(flag, v[:, :blk], v[:, blk:])
        give[...] = jnp.where(flag, v[:, blk:], v[:, :blk])

    return call(body, (x, ps, ra, rb, sc, pos), [((blk, blk), f32)] * 2, 1 << 20)


def stack(keep, got, pos):
    blk = keep.shape[0]

    def body(keep, got, pos, o):
        core = pos[2] % 2
        o[pl.ds(pl.multiple_of(core * blk, blk), blk), :] = keep[...]
        o[pl.ds(pl.multiple_of(blk - core * blk, blk), blk), :] = got[...]

    return call(body, (keep, got, pos), [((2 * blk, blk), f32)], 1 << 20)[0]


def per_device(x, observed, fx, bx, fy, by, step_size, threshold):
    blk = fx.shape[2]
    rows, cols = lax.axis_size("row"), lax.axis_size("col")
    chips = cols // 2
    at = lambda r, c: r * cols + c
    both = lambda forth: forth + [(j, i) for i, j in forth]
    chip_pairs = both([(2 * k, 2 * k + 1) for k in range(chips)])
    outer_pairs = both([(2 * k + 1, 2 * k + 2) for k in range(chips - 1)])
    side_pairs = [
        both([(2 * k + i, 2 * k + 2 + i) for k in range(first, chips - 1, 2) for i in range(2)])
        for first in (0, 1)
    ]
    row_pairs = both(
        [(at(r, 2 * k), at(r - 1, 2 * k + 1)) for r in range(1, rows) for k in range(chips)]
    )
    same_core = [(at(r, 2 * k), at(r + 1, 2 * k)) for r in range(rows - 1) for k in range(chips)]
    same_core += [(at(r, 2 * k + 1), at(r - 1, 2 * k + 1)) for r in range(1, rows) for k in range(chips)]

    swap_chip = lambda v: lax.ppermute(v, "col", chip_pairs)
    swap_row = lambda v: lax.ppermute(v, ("row", "col"), row_pairs)

    def swap_sides(e, o):
        ro = lax.ppermute(o, "col", side_pairs[1])
        re = lax.ppermute(e, "col", side_pairs[0])
        return re, ro

    col = lax.axis_index("col")
    core = col % 2
    pos = jnp.stack([lax.axis_index("row"), rows, col, cols]).astype(jnp.int32)
    sc = jnp.concatenate([step_size, threshold])
    mine = lax.dynamic_slice_in_dim(x, core * blk, blk)
    other = lax.dynamic_slice_in_dim(x, blk - core * blk, blk)
    bother = swap_row(mine)
    bown = lax.ppermute(other, ("row", "col"), same_core)
    xp = swap_chip(x)
    obsp = swap_chip(lax.dynamic_slice_in_dim(observed, blk - core * blk, blk))
    ax, atx, own, outer = prepare(fx, bx, fy, by, pos)
    gown = lax.ppermute(outer, "col", outer_pairs)
    gother = swap_chip(gown[:blk])
    fw, fn, fe, fo = prepare_columns(own, swap_chip(own), pos)

    e, o, x, obs = first_messages(x, xp, bown, bother, observed, obsp, ax, fw, pos)
    re, ro = swap_sides(e, o)
    ps, pa, pb = back(e, o, re, ro, gown, gother, fe, fo, fn, atx, pos)
    x = update(x, ps, swap_chip(pa), swap_row(pb), sc)
    e, o = later_messages(x, swap_chip(x), swap_row(x), obs, ax, fw)
    re, ro = swap_sides(e, o)
    ps, pa, pb = back(e, o, re, ro, gown, gother, fe, fo, fn, atx, pos)
    keep, give = last_update(x, ps, swap_chip(pa), swap_row(pb), sc, pos)
    return stack(keep, swap_chip(give), pos)


def solution(mesh):
    in_specs = (
        P("row", "col"),
        P("row", "col"),
        P("row", None, None, None),
        P("row", None),
        P("col", None, None, None),
        P("col", None),
        P(),
        P(),
    )
    return jax.shard_map(
        per_device, mesh=mesh, in_specs=in_specs, out_specs=P("row", "col"), check_vma=False
    )
```

```python
import jax
import jax.numpy as jnp
from jax import lax
from jax.experimental import pallas as pl
from jax.experimental.pallas import tpu as pltpu
from jax.sharding import PartitionSpec as P


f32 = jnp.float32
bf16 = jnp.bfloat16
VMEM = pl.BlockSpec(memory_space=pltpu.VMEM)
SMEM = pl.BlockSpec(memory_space=pltpu.SMEM)


def split(x):
    hi = x.astype(bf16)
    return hi, (x - hi.astype(f32)).astype(bf16)


def dot3(x, y):
    (xh, xl), (yh, yl) = x, y
    mm = lambda a, b: jnp.dot(a, b, preferred_element_type=f32)
    return mm(xh, yh) + (mm(xh, yl) + mm(xl, yh))


def soft(v, h):
    return v - jnp.minimum(jnp.maximum(v, -h), h)


def call(body, ins, outs, flops, scratch=(), limit=16 << 20):
    size = lambda a: a.size * a.dtype.itemsize
    return pl.pallas_call(
        body,
        out_shape=[jax.ShapeDtypeStruct(s, d) for s, d in outs],
        in_specs=[SMEM if a.size < 64 else VMEM for a in ins],
        out_specs=[VMEM for _ in outs],
        scratch_shapes=list(scratch),
        compiler_params=pltpu.CompilerParams(vmem_limit_bytes=limit),
        cost_estimate=pl.CostEstimate(
            flops=flops, bytes_accessed=sum(size(a) for a in ins), transcendentals=0
        ),
    )(*ins)


def own_is_e(pos):
    return (pos[2] // 2 + pos[2] % 2) % 2 == 1


def prepare(fx, bx, pos):
    blk = fx.shape[2]

    def body(fx, bx, pos, ah, al, th, tl):
        row, rows, core = pos[0], pos[1], pos[2] % 2
        for k, s in enumerate((1, 2 - 2 * core, 2 * core)):
            r = slice(k * blk, (k + 1) * blk)
            m = bx[core, s].astype(f32)
            if k == 2:
                m = jnp.where(row == jnp.where(core == 0, 0, rows - 1), 0.0, m)
            v = fx[core, s] * m
            ah[:, r], al[:, r] = split(v)
            th[r, :], tl[r, :] = split(v.T)

    outs = [((blk, 3 * blk), bf16)] * 2 + [((3 * blk, blk), bf16)] * 2
    o = call(body, (fx, bx, pos), outs, 0)
    return o[0:2], o[2:4]


def prepare_columns(own, other, pos):
    blk = own.shape[2]

    def body(own, other, pos, wh, wl, nh, nl, eh, el, oh, ol):
        flag = own_is_e(pos)
        core = pos[2] % 2

        def pick(i):
            p = own[(1, 2 - 2 * core, 2 * core)[i]]
            k = (1, 2 * core, 2 - 2 * core)[i]
            q = other[pl.ds(pl.multiple_of(k * blk, blk), blk), :]
            return jnp.where(flag, p, q), jnp.where(flag, q, p)

        (ee, oo), (eo, oe), (ex, ox) = pick(0), pick(1), pick(2)
        a, b = slice(0, blk), slice(blk, 2 * blk)
        for v, i, j in ((ee, a, a), (eo, a, b), (oo, b, b), (oe, b, a)):
            nh[i, j], nl[i, j] = split(v)
            wh[j, i], wl[j, i] = split(v.T)
        eh[...], el[...] = split(ex.T)
        oh[...], ol[...] = split(ox.T)

    outs = [((2 * blk, 2 * blk), bf16)] * 4 + [((blk, blk), bf16)] * 4
    o = call(body, (own, other, pos), outs, 0)
    return o[0:2], o[2:4], o[4:6], o[6:8]


def messages(xh, xl, ah, al, wh, wl, obs, e, o, o2):
    blk = ah.shape[0]
    u = dot3((ah[...], al[...]), (xh[...], xl[...]))
    w = dot3(split(u), (wh[...], wl[...])) - obs
    cut = o.shape[0] - blk
    a, b = slice(0, blk), slice(blk, 2 * blk)
    e[:blk, :], e[blk:, :] = u[:, a], w[:, a]
    o[:blk, :], o[blk:, :] = u[:, b], w[:cut, b]
    o2[...] = w[cut:, b]


def message_shapes(blk):
    cut = blk // 4
    return [((2 * blk, blk), f32), ((blk + cut, blk), f32), ((blk - cut, blk), f32)]


def first_messages(x, packed, bown, bother, obs, ax, fw, pos):
    m, blk = x.shape

    def body(x, pk, bown, bother, obs, ah, al, wh, wl, pos, e, o, o2, x0, ob, xh, xl):
        flag = own_is_e(pos)
        core = pos[2] % 2
        at = lambda first: pl.ds(pl.multiple_of(first, blk), blk)
        here, there = core * blk, blk - core * blk
        rows = ((x[at(here), :], pk[at(3 * blk + here), :]), (x[at(there), :], pk[at(3 * blk + there), :]))
        rows += ((bown[...], bother[...]),)
        a, b = slice(0, blk), slice(blk, 2 * blk)
        for k, (p, q) in enumerate(rows):
            r = slice(k * blk, (k + 1) * blk)
            ve, vo = jnp.where(flag, p, q), jnp.where(flag, q, p)
            if k == 0:
                x0[:, a], x0[:, b] = ve, vo
            xh[r, a], xl[r, a] = split(ve)
            xh[r, b], xl[r, b] = split(vo)
        p, q = obs[at(here), :], pk[5 * blk :, :]
        ob[:, a], ob[:, b] = jnp.where(flag, p, q), jnp.where(flag, q, p)
        messages(xh, xl, ah, al, wh, wl, ob[...], e, o, o2)

    outs = message_shapes(blk) + [((blk, 2 * blk), f32)] * 2
    scratch = [pltpu.VMEM((3 * blk, 2 * blk), bf16)] * 2
    ins = (x, packed, bown, bother, obs, *ax, *fw, pos)
    return call(body, ins, outs, 60 * blk**3, scratch)


def later_messages(x, xa, xb, obs, ax, fw):
    blk = x.shape[0]

    def body(x, xa, xb, obs, ah, al, wh, wl, e, o, o2, xh, xl):
        for k, v in enumerate((x, xa, xb)):
            r = slice(k * blk, (k + 1) * blk)
            xh[r, :], xl[r, :] = split(v[...])
        messages(xh, xl, ah, al, wh, wl, obs[...], e, o, o2)

    scratch = [pltpu.VMEM((3 * blk, 2 * blk), bf16)] * 2
    return call(body, (x, xa, xb, obs, *ax, *fw), message_shapes(blk), 60 * blk**3, scratch)


def back(sent, got, gown, gother, fe, fo, fn, atx, pos):
    blk = sent[0].shape[1]

    def body(e, o, o2, re, ro, ro2, relayed, gown, gother, eh, el, oh, ol, nh, nl, th, tl, pos, ps, pa, pb, mh, ml):
        flag = own_is_e(pos)
        half = pos[3] // 4
        chip = pos[2] // 2
        middle = (chip == half - 1) | (chip == half)
        gp, gq = gown[:blk, :], gother[...]
        join = lambda a, b: jnp.concatenate([a[blk:, :], b], axis=0)
        tail = jnp.where(middle, relayed[...], ro2[...])
        sides = (
            (e, e[blk:, :], re, re[blk:, :], (eh, el), jnp.where(flag, gp, gq), slice(0, blk)),
            (o, join(o, o2[...]), ro, join(ro, tail), (oh, ol), jnp.where(flag, gq, gp), slice(blk, 2 * blk)),
        )
        outer = []
        for u, w, ru, rw, (fh, fl), g, s in sides:
            m = w + dot3(split(ru[:blk, :]), (fh[...], fl[...]))
            mh[:, s], ml[:, s] = split(m)
            beyond = rw + dot3(split(u[:blk, :]), split(g.T))
            outer.append(dot3(split(beyond), split(g)))
        n = dot3((mh[...], ml[...]), (nh[...], nl[...])) + jnp.concatenate(outer, axis=1)
        nsplit = split(n)
        for k, out in enumerate((ps, pa, pb)):
            r = slice(k * blk, (k + 1) * blk)
            out[...] = dot3((th[r, :], tl[r, :]), nsplit)

    scratch = [pltpu.VMEM((blk, 2 * blk), bf16)] * 2
    ins = (*sent, *got, gown, gother, *fe, *fo, *fn, *atx, pos)
    return call(body, ins, [((blk, 2 * blk), f32)] * 3, 96 * blk**3, scratch)


def update(x, ps, ra, rb, sc):
    def body(x, ps, ra, rb, sc, o):
        o[...] = soft(x[...] - sc[0] * (ps[...] + (ra[...] + rb[...])), sc[1])

    return call(body, (x, ps, ra, rb, sc), [(x.shape, f32)], 1 << 20)[0]


def last_update(x, ps, ra, rb, sc, pos):
    blk = x.shape[0]

    def body(x, ps, ra, rb, sc, pos, keep, give):
        flag = own_is_e(pos)
        v = soft(x[...] - sc[0] * (ps[...] + (ra[...] + rb[...])), sc[1])
        keep[...] = jnp.where(flag, v[:, :blk], v[:, blk:])
        give[...] = jnp.where(flag, v[:, blk:], v[:, :blk])

    return call(body, (x, ps, ra, rb, sc, pos), [((blk, blk), f32)] * 2, 1 << 20)


def stack(keep, got, pos):
    blk = keep.shape[0]

    def body(keep, got, pos, o):
        core = pos[2] % 2
        o[pl.ds(pl.multiple_of(core * blk, blk), blk), :] = keep[...]
        o[pl.ds(pl.multiple_of(blk - core * blk, blk), blk), :] = got[...]

    return call(body, (keep, got, pos), [((2 * blk, blk), f32)], 1 << 20)[0]


def per_device(x, observed, fx, bx, fy, by, step_size, threshold):
    blk = fx.shape[2]
    rows, cols = lax.axis_size("row"), lax.axis_size("col")
    chips = cols // 2
    at = lambda r, c: r * cols + c
    both = lambda forth: forth + [(j, i) for i, j in forth]
    chip_pairs = both([(2 * k, 2 * k + 1) for k in range(chips)])
    outer_pairs = both([(2 * k + 1, 2 * k + 2) for k in range(chips - 1)])
    side_pairs = [
        both([(2 * k + i, 2 * k + 2 + i) for k in range(first, chips - 1, 2) for i in range(2)])
        for first in (0, 1)
    ]
    row_pairs = both(
        [(at(r, 2 * k), at(r - 1, 2 * k + 1)) for r in range(1, rows) for k in range(chips)]
    )
    same_core = [(at(r, 2 * k), at(r + 1, 2 * k)) for r in range(rows - 1) for k in range(chips)]
    same_core += [(at(r, 2 * k + 1), at(r - 1, 2 * k + 1)) for r in range(1, rows) for k in range(chips)]

    half = chips // 2
    cores = lambda hops: [(2 * i + c, 2 * j + c) for i, j in hops for c in range(2)]
    first_hop = [p for p in side_pairs[1] if {p[0] // 2, p[1] // 2} != {half - 1, half}]
    first_hop += cores([(half - 1, 0), (half, chips - 1)])
    second_hop = cores([(0, half), (chips - 1, half - 1)])

    swap_chip = lambda v: lax.ppermute(v, "col", chip_pairs)
    swap_row = lambda v: lax.ppermute(v, ("row", "col"), row_pairs)

    def swap_sides(e, o, o2):
        ro2 = lax.ppermute(o2, "col", first_hop)
        ro = lax.ppermute(o, "col", side_pairs[1])
        re = lax.ppermute(e, "col", side_pairs[0])
        return re, ro, ro2, lax.ppermute(ro2, "col", second_hop)

    col = lax.axis_index("col")
    core = col % 2
    pos = jnp.stack([lax.axis_index("row"), rows, col, cols]).astype(jnp.int32)
    sc = jnp.concatenate([step_size, threshold])
    mine = lax.dynamic_slice_in_dim(x, core * blk, blk)
    other = lax.dynamic_slice_in_dim(x, blk - core * blk, blk)
    bother = swap_row(mine)
    bown = lax.ppermute(other, ("row", "col"), same_core)
    slot = jnp.arange(3)
    inside = ((slot > 0) | (col > 0)) & ((slot < 2) | (col < cols - 1))
    fy = fy[0] * (by[0] * inside).astype(f32)[:, None, None]
    far = lax.dynamic_slice_in_dim(observed, blk - core * blk, blk)
    packed = swap_chip(jnp.concatenate([fy.reshape(3 * blk, blk), x, far]))
    outer = lax.dynamic_slice_in_dim(fy, 2 * core, 1)[0]
    gown = lax.ppermute(jnp.pad(outer, ((0, blk + 8), (0, 0))), "col", outer_pairs)
    gother = swap_chip(gown[:blk])
    ax, atx = prepare(fx, bx, pos)
    fw, fn, fe, fo = prepare_columns(fy, packed, pos)

    *sent, x, obs = first_messages(x, packed, bown, bother, observed, ax, fw, pos)
    got = swap_sides(*sent)
    ps, pa, pb = back(sent, got, gown, gother, fe, fo, fn, atx, pos)
    x = update(x, ps, swap_chip(pa), swap_row(pb), sc)
    sent = later_messages(x, swap_chip(x), swap_row(x), obs, ax, fw)
    got = swap_sides(*sent)
    ps, pa, pb = back(sent, got, gown, gother, fe, fo, fn, atx, pos)
    keep, give = last_update(x, ps, swap_chip(pa), swap_row(pb), sc, pos)
    return stack(keep, swap_chip(give), pos)


def solution(mesh):
    in_specs = (
        P("row", "col"),
        P("row", "col"),
        P("row", None, None, None),
        P("row", None),
        P("col", None, None, None),
        P("col", None),
        P(),
        P(),
    )
    return jax.shard_map(
        per_device, mesh=mesh, in_specs=in_specs, out_specs=P("row", "col"), check_vma=False
    )
```

```python
import jax
import jax.numpy as jnp
from jax import lax
from jax.experimental import pallas as pl
from jax.experimental.pallas import tpu as pltpu
from jax.sharding import PartitionSpec as P

f32 = jnp.float32
bf16 = jnp.bfloat16
VMEM = pl.BlockSpec(memory_space=pltpu.VMEM)
SMEM = pl.BlockSpec(memory_space=pltpu.SMEM)
CHUNK = 256


def split(x):
    hi = x.astype(bf16)
    return hi, (x - hi.astype(f32)).astype(bf16)


def dot3(xh, xl, yh, yl):
    mm = lambda a, b: jnp.dot(a, b, preferred_element_type=f32)
    return mm(xh, yh) + (mm(xh, yl) + mm(xl, yh))


def soft(v, h):
    return v - jnp.minimum(jnp.maximum(v, -h), h)


def call(body, ins, outs, flops, scratch=(), limit=24 << 20):
    size = lambda a: a.size * a.dtype.itemsize
    return pl.pallas_call(
        body,
        out_shape=[jax.ShapeDtypeStruct(s, d) for s, d in outs],
        in_specs=[SMEM if a.size < 64 else VMEM for a in ins],
        out_specs=[VMEM for _ in outs],
        scratch_shapes=list(scratch),
        compiler_params=pltpu.CompilerParams(vmem_limit_bytes=limit),
        cost_estimate=pl.CostEstimate(
            flops=flops, bytes_accessed=sum(size(a) for a in ins), transcendentals=0
        ),
    )(*ins)


def prepare(fx, bx, fy, by, pos):
    blk = fx.shape[2]

    def body(fx, bx, fy, by, pos, axh, axl, atxh, atxl, byh, byl, byth, bytl, fb):
        row, rows, col, cols = pos[0], pos[1], pos[2], pos[3]

        def put(v, k, plain, trans):
            s = slice(k * blk, (k + 1) * blk)
            plain[0][:, s], plain[1][:, s] = split(v)
            trans[0][s, :], trans[1][s, :] = split(v.T)

        for r in range(2):
            for s in range(3):
                m = bx[r, s].astype(f32)
                if (r, s) == (0, 0):
                    m = jnp.where(row == 0, 0.0, m)
                if (r, s) == (1, 2):
                    m = jnp.where(row == rows - 1, 0.0, m)
                put(fx[r, s] * m, s, (axh.at[r], axl.at[r]), (atxh.at[r], atxl.at[r]))
        first = jnp.where(col % 2 == 0, 2, 0)
        for k, s in enumerate((first, 1, 2 - first)):
            m = by[0, s].astype(f32)
            m = jnp.where((s == 0) & (col == 0), 0.0, m)
            m = jnp.where((s == 2) & (col == cols - 1), 0.0, m)
            v = fy[0, s] * m
            put(v, k, (byh, byl), (byth, bytl))
        fb[...] = v

    outs = [((2, blk, 3 * blk), bf16)] * 2 + [((2, 3 * blk, blk), bf16)] * 2
    outs += [((blk, 3 * blk), bf16)] * 2 + [((3 * blk, blk), bf16)] * 2
    outs += [((blk, blk), f32)]
    o = call(body, (fx, bx, fy, by, pos), outs, 1 << 24)
    return o[0:2], o[2:4], o[4:6], o[6:8], o[8]


def left(ax, xs, u):
    blk = xs[0].shape[0] // 4
    for r in range(2):
        s = slice(r * blk, (r + 3) * blk)
        u[r * blk : (r + 1) * blk, :] = dot3(ax[0][r], ax[1][r], xs[0][s, :], xs[1][s, :])


def apply_left(x, up, down, ax):
    blk, n = up.shape

    def body(x, up, down, axh, axl, u, xh, xl):
        for t, v in enumerate((up[...], x[:blk, :], x[blk:, :], down[...])):
            s = slice(t * blk, (t + 1) * blk)
            xh[s, :], xl[s, :] = split(v)
        left((axh, axl), (xh, xl), u)

    scratch = [pltpu.VMEM((4 * blk, n), bf16)] * 2
    return call(body, (x, up, down, *ax), [(x.shape, f32)], 36 * blk * blk * n, scratch)[0]


def rows_of(first, second, r):
    cut, (a, b) = first.shape[0], r
    parts = []
    if a < cut:
        parts.append(first[a : min(b, cut), :])
    if b > cut:
        parts.append(second[max(a - cut, 0) : b - cut, :])
    return parts[0] if len(parts) == 1 else jnp.concatenate(parts, axis=0)


def near_misfit(u, ua, observed, byt, below, cut):
    m, blk = u.shape
    extra = below.shape[0]

    def body(u, ua, obs, byth, bytl, below, w, v):
        v[m - cut :, :] = below[...]
        for i in range(0, m, CHUNK):
            r = slice(i, i + CHUNK)
            acc = -obs[r, :]
            for k, x in enumerate((ua, u)):
                s = slice(k * blk, (k + 1) * blk)
                acc = acc + dot3(*split(x[r, :]), byth[s, :], bytl[s, :])
            here = min(max(cut - i, 0), CHUNK)
            if here:
                w[i : i + here, :] = acc[:here]
            if here < CHUNK:
                v[i + here - cut : i + CHUNK - cut, :] = acc[here:]

    outs = [((cut, blk), f32), ((m - cut + extra, blk), f32)]
    return call(body, (u, ua, observed, *byt, below), outs, 24 * m * blk * blk)


def full_misfit(w, v, ub, byt, by):
    m, blk = ub.shape

    def body(w, v, ub, byth, bytl, byh, byl, qa, qa2, q):
        b = slice(2 * blk, 3 * blk)
        for i, qa in ((0, qa), (m // 2, qa2)):
            r = slice(i, i + m // 2)
            acc = rows_of(w, v, (i, i + m // 2)) + dot3(*split(ub[r, :]), byth[b, :], bytl[b, :])
            mh, ml = split(acc)
            qa[...] = dot3(mh, ml, byh[:, :blk], byl[:, :blk])
            q[r, :] = dot3(mh, ml, byh[:, blk : 2 * blk], byl[:, blk : 2 * blk])

    outs = [((m // 2, blk), f32)] * 2 + [((m, blk), f32)]
    return call(body, (w, v, ub, *byt, *by), outs, 36 * m * blk * blk)


def back(q, ra, ra2, wb, vb, relayed, u, fb, atx, pos, merged):
    m, n = q.shape
    blk = m // 2
    cut = wb.shape[0]
    ins = (q, ra, ra2, wb, vb, relayed, u, *([] if merged else [fb]), *atx, pos)

    def body(q, ra, ra2, wb, vb, relayed, u, *rest):
        fb = None
        if not merged:
            fb, *rest = rest
        ah, al, pos, *outs = rest
        half = pos[3] // 2
        special = (pos[2] == half - 1) | (pos[2] == half) | (pos[2] == 0) | (pos[2] == pos[3] - 1)
        tail = jnp.where(special, relayed[...], vb[...])
        if merged:
            *outs, keep = outs
            g = tail[m - cut : m - cut + blk]
            keep[...] = g
        else:
            g = fb[...]
        gh, gl = split(g)
        th, tl = split(g.T)
        p = []
        for r, a in ((0, ra), (1, ra2)):
            s = slice(r * blk, (r + 1) * blk)
            other = rows_of(wb, tail, (r * blk, (r + 1) * blk)) + dot3(*split(u[s, :]), th, tl)
            v = q[s, :] + a[...] + dot3(*split(other), gh, gl)
            p.append(dot3(ah[r], al[r], *split(v)))
        p0 = p[0][:blk]
        p1 = p[0][blk : 2 * blk] + p[1][:blk]
        p2 = p[0][2 * blk :] + p[1][blk : 2 * blk]
        p3 = p[1][2 * blk :]
        if merged:
            top, bottom = outs
            top[:blk, :], top[blk:, :] = p0, p1
            bottom[:blk, :], bottom[blk:, :] = p2, p3
        else:
            top, mid, bottom = outs
            top[...], bottom[...] = p0, p3
            mid[:blk, :], mid[blk:, :] = p1, p2

    outs = [((m, n), f32)] * 2 if merged else [((blk, n), f32), ((m, n), f32)]
    return call(body, ins, outs + [((blk, n), f32)], 60 * blk * blk * n)


def update_left(top, bottom, rtop, rbottom, x, up, down, sc, ax):
    blk, n = up.shape

    def body(top, bottom, rtop, rbottom, x, up, down, sc, axh, axl, xn, u, xh, xl):
        step, h = sc[0], sc[1]
        lo, hi = slice(0, blk), slice(blk, 2 * blk)
        parts = ((up[...], top, rtop, lo), (x[lo, :], top, rtop, hi))
        parts += ((x[hi, :], bottom, rbottom, lo), (down[...], bottom, rbottom, hi))
        for t, (v, a, b, s) in enumerate(parts):
            new = soft(v - step * (a[s, :] + b[s, :]), h)
            if t in (1, 2):
                xn[(t - 1) * blk : t * blk, :] = new
            d = slice(t * blk, (t + 1) * blk)
            xh[d, :], xl[d, :] = split(new)
        left((axh, axl), (xh, xl), u)

    scratch = [pltpu.VMEM((4 * blk, n), bf16)] * 2
    ins = (top, bottom, rtop, rbottom, x, up, down, sc, *ax)
    return call(body, ins, [(x.shape, f32)] * 2, 36 * blk * blk * n, scratch)


def update(mid, rup, rdown, x, sc):
    blk, n = rup.shape

    def body(mid, rup, rdown, x, sc, o):
        step, h = sc[0], sc[1]
        lo, hi = slice(0, blk), slice(blk, 2 * blk)
        for s, r in ((lo, rup), (hi, rdown)):
            o[s, :] = soft(x[s, :] - step * (mid[s, :] + r[...]), h)

    return call(body, (mid, rup, rdown, x, sc), [(x.shape, f32)], 1 << 20)[0]


def per_device(x, observed, fx, bx, fy, by, step_size, threshold):
    blk = fx.shape[2]
    rows, cols = lax.axis_size("row"), lax.axis_size("col")
    downward = [(i, i + 1) for i in range(rows - 1)]
    upward = [(i + 1, i) for i in range(rows - 1)]
    pairs = []
    for first in (0, 1):
        forth = [(i, i + 1) for i in range(first, cols - 1, 2)]
        pairs.append(forth + [(j, i) for i, j in forth])

    def row_swap(to_up, to_down):
        from_up = lax.ppermute(to_down, "row", downward)
        from_down = lax.ppermute(to_up, "row", upward)
        return from_up, from_down

    def chip_swap(a):
        return lax.ppermute(a, "col", pairs[0])

    def col_swap(b):
        return lax.ppermute(b, "col", pairs[1])

    half = cols // 2
    first_hop = [p for p in pairs[1] if set(p) != {half - 1, half}] + [(half - 1, 0), (half, cols - 1)]
    second_hop = [(0, half), (cols - 1, half - 1)]

    def columns(u, fb, merged):
        ua = chip_swap(u)
        ub = col_swap(u)
        if merged:
            w, v = near_misfit(u, ua, observed, byt, fb, 7 * blk // 4)
        else:
            pad = jnp.zeros((16, fb.shape[1]), f32)
            w, v = near_misfit(u, ua, observed, byt, pad, blk + 8)
        vb = lax.ppermute(v, "col", first_hop)
        wb = col_swap(w)
        relayed = lax.ppermute(vb, "col", second_hop)
        qa, qa2, q = full_misfit(w, v, ub, byt, byf)
        ra, ra2 = chip_swap(qa), chip_swap(qa2)
        return back(q, ra, ra2, wb, vb, relayed, u, fb, atx, pos, merged)

    pos = jnp.stack([lax.axis_index("row"), rows, lax.axis_index("col"), cols]).astype(jnp.int32)
    sc = jnp.concatenate([step_size, threshold])
    up, down = row_swap(x[:blk], x[blk:])
    ax, atx, byf, byt, fb = prepare(fx, bx, fy, by, pos)
    u = apply_left(x, up, down, ax)
    top, bottom, fb = columns(u, fb, True)
    rtop, rbottom = row_swap(top, bottom)
    x, u = update_left(top, bottom, rtop, rbottom, x, up, down, sc, ax)
    top, mid, bottom = columns(u, fb, False)
    rup, rdown = row_swap(top, bottom)
    return update(mid, rup, rdown, x, sc)


def solution(mesh):
    in_specs = (
        P("row", "col"),
        P("row", "col"),
        P("row", None, None, None),
        P("row", None),
        P("col", None, None, None),
        P("col", None),
        P(),
        P(),
    )
    return jax.shard_map(
        per_device, mesh=mesh, in_specs=in_specs, out_specs=P("row", "col"), check_vma=False
    )
```

```python
import jax
import jax.numpy as jnp
from jax import lax
from jax.experimental import pallas as pl
from jax.experimental.pallas import tpu as pltpu
from jax.sharding import PartitionSpec as P

f32 = jnp.float32
bf16 = jnp.bfloat16
VMEM = pl.BlockSpec(memory_space=pltpu.VMEM)
SMEM = pl.BlockSpec(memory_space=pltpu.SMEM)
CHUNK = 256


def split(x):
    hi = x.astype(bf16)
    return hi, (x - hi.astype(f32)).astype(bf16)


def dot3(xh, xl, yh, yl):
    mm = lambda a, b: jnp.dot(a, b, preferred_element_type=f32)
    return mm(xh, yh) + (mm(xh, yl) + mm(xl, yh))


def soft(v, h):
    return v - jnp.minimum(jnp.maximum(v, -h), h)


def call(body, ins, outs, flops, scratch=(), limit=24 << 20):
    size = lambda a: a.size * a.dtype.itemsize
    return pl.pallas_call(
        body,
        out_shape=[jax.ShapeDtypeStruct(s, d) for s, d in outs],
        in_specs=[SMEM if a.size < 64 else VMEM for a in ins],
        out_specs=[VMEM for _ in outs],
        scratch_shapes=list(scratch),
        compiler_params=pltpu.CompilerParams(vmem_limit_bytes=limit),
        cost_estimate=pl.CostEstimate(
            flops=flops, bytes_accessed=sum(size(a) for a in ins), transcendentals=0
        ),
    )(*ins)


def prepare(fx, bx, fy, by, pos):
    blk = fx.shape[2]

    def body(fx, bx, fy, by, pos, axh, axl, atxh, atxl, byh, byl, byth, bytl, fb):
        row, rows, col, cols = pos[0], pos[1], pos[2], pos[3]

        def put(v, k, plain, trans):
            s = slice(k * blk, (k + 1) * blk)
            plain[0][:, s], plain[1][:, s] = split(v)
            trans[0][s, :], trans[1][s, :] = split(v.T)

        for r in range(2):
            for s in range(3):
                m = bx[r, s].astype(f32)
                if (r, s) == (0, 0):
                    m = jnp.where(row == 0, 0.0, m)
                if (r, s) == (1, 2):
                    m = jnp.where(row == rows - 1, 0.0, m)
                put(fx[r, s] * m, s, (axh.at[r], axl.at[r]), (atxh.at[r], atxl.at[r]))
        first = jnp.where(col % 2 == 0, 2, 0)
        for k, s in enumerate((first, 1, 2 - first)):
            m = by[0, s].astype(f32)
            m = jnp.where((s == 0) & (col == 0), 0.0, m)
            m = jnp.where((s == 2) & (col == cols - 1), 0.0, m)
            v = fy[0, s] * m
            put(v, k, (byh, byl), (byth, bytl))
        fb[...] = v

    outs = [((2, blk, 3 * blk), bf16)] * 2 + [((2, 3 * blk, blk), bf16)] * 2
    outs += [((blk, 3 * blk), bf16)] * 2 + [((3 * blk, blk), bf16)] * 2
    outs += [((blk, blk), f32)]
    o = call(body, (fx, bx, fy, by, pos), outs, 1 << 24)
    return o[0:2], o[2:4], o[4:6], o[6:8], o[8]


def left(ax, xs, u):
    blk = xs[0].shape[0] // 4
    for r in range(2):
        s = slice(r * blk, (r + 3) * blk)
        u[r * blk : (r + 1) * blk, :] = dot3(ax[0][r], ax[1][r], xs[0][s, :], xs[1][s, :])


def apply_left(x, up, down, ax):
    blk, n = up.shape

    def body(x, up, down, axh, axl, u, xh, xl):
        for t, v in enumerate((up[...], x[:blk, :], x[blk:, :], down[...])):
            s = slice(t * blk, (t + 1) * blk)
            xh[s, :], xl[s, :] = split(v)
        left((axh, axl), (xh, xl), u)

    scratch = [pltpu.VMEM((4 * blk, n), bf16)] * 2
    return call(body, (x, up, down, *ax), [(x.shape, f32)], 36 * blk * blk * n, scratch)[0]


def rows_of(first, second, r):
    cut, (a, b) = first.shape[0], r
    parts = []
    if a < cut:
        parts.append(first[a : min(b, cut), :])
    if b > cut:
        parts.append(second[max(a - cut, 0) : b - cut, :])
    return parts[0] if len(parts) == 1 else jnp.concatenate(parts, axis=0)


def near_misfit(u, ua, observed, byt, below, cut):
    m, blk = u.shape
    extra = below.shape[0]

    def body(u, ua, obs, byth, bytl, below, w, v):
        v[m - cut :, :] = below[...]
        for i in range(0, m, CHUNK):
            r = slice(i, i + CHUNK)
            acc = -obs[r, :]
            for k, x in enumerate((ua, u)):
                s = slice(k * blk, (k + 1) * blk)
                acc = acc + dot3(*split(x[r, :]), byth[s, :], bytl[s, :])
            here = min(max(cut - i, 0), CHUNK)
            if here:
                w[i : i + here, :] = acc[:here]
            if here < CHUNK:
                v[i + here - cut : i + CHUNK - cut, :] = acc[here:]

    outs = [((cut, blk), f32), ((m - cut + extra, blk), f32)]
    return call(body, (u, ua, observed, *byt, below), outs, 24 * m * blk * blk)


def full_misfit(w, v, ub, byt, by):
    m, blk = ub.shape

    def body(w, v, ub, byth, bytl, byh, byl, qa, qa2, q):
        b = slice(2 * blk, 3 * blk)
        for i, qa in ((0, qa), (m // 2, qa2)):
            r = slice(i, i + m // 2)
            acc = rows_of(w, v, (i, i + m // 2)) + dot3(*split(ub[r, :]), byth[b, :], bytl[b, :])
            mh, ml = split(acc)
            qa[...] = dot3(mh, ml, byh[:, :blk], byl[:, :blk])
            q[r, :] = dot3(mh, ml, byh[:, blk : 2 * blk], byl[:, blk : 2 * blk])

    outs = [((m // 2, blk), f32)] * 2 + [((m, blk), f32)]
    return call(body, (w, v, ub, *byt, *by), outs, 36 * m * blk * blk)


def back(q, ra, ra2, wb, vb, relayed, u, fb, atx, pos, merged):
    m, n = q.shape
    blk = m // 2
    cut = wb.shape[0]
    ins = (q, ra, ra2, wb, vb, relayed, u, *(() if merged else fb), *atx, pos)

    def body(q, ra, ra2, wb, vb, relayed, u, *rest):
        if merged:
            ah, al, pos, *outs = rest
        else:
            gh, gl, th, tl, ah, al, pos, *outs = rest
        half = pos[3] // 2
        special = (pos[2] == half - 1) | (pos[2] == half) | (pos[2] == 0) | (pos[2] == pos[3] - 1)
        tail = jnp.where(special, relayed[...], vb[...])
        if merged:
            *outs, gh, gl, th, tl = outs
            g = tail[m - cut : m - cut + blk]
            gh[...], gl[...] = split(g)
            th[...], tl[...] = split(g.T)
        block, flipped = (gh[...], gl[...]), (th[...], tl[...])
        p = []
        for r, a in ((0, ra), (1, ra2)):
            s = slice(r * blk, (r + 1) * blk)
            other = rows_of(wb, tail, (r * blk, (r + 1) * blk)) + dot3(*split(u[s, :]), *flipped)
            v = q[s, :] + a[...] + dot3(*split(other), *block)
            p.append(dot3(ah[r], al[r], *split(v)))
        p0 = p[0][:blk]
        p1 = p[0][blk : 2 * blk] + p[1][:blk]
        p2 = p[0][2 * blk :] + p[1][blk : 2 * blk]
        p3 = p[1][2 * blk :]
        if merged:
            top, bottom = outs
            top[:blk, :], top[blk:, :] = p0, p1
            bottom[:blk, :], bottom[blk:, :] = p2, p3
        else:
            top, mid, bottom = outs
            top[...], bottom[...] = p0, p3
            mid[:blk, :], mid[blk:, :] = p1, p2

    if merged:
        outs = [((m, n), f32)] * 2 + [((n, n), bf16)] * 4
    else:
        outs = [((blk, n), f32), ((m, n), f32), ((blk, n), f32)]
    return call(body, ins, outs, 60 * blk * blk * n)


def update_left(top, bottom, rtop, rbottom, x, up, down, sc, ax):
    blk, n = up.shape

    def body(top, bottom, rtop, rbottom, x, up, down, sc, axh, axl, xn, u, xh, xl):
        step, h = sc[0], sc[1]
        lo, hi = slice(0, blk), slice(blk, 2 * blk)
        parts = ((up[...], top, rtop, lo), (x[lo, :], top, rtop, hi))
        parts += ((x[hi, :], bottom, rbottom, lo), (down[...], bottom, rbottom, hi))
        for t, (v, a, b, s) in enumerate(parts):
            new = soft(v - step * (a[s, :] + b[s, :]), h)
            if t in (1, 2):
                xn[(t - 1) * blk : t * blk, :] = new
            d = slice(t * blk, (t + 1) * blk)
            xh[d, :], xl[d, :] = split(new)
        left((axh, axl), (xh, xl), u)

    scratch = [pltpu.VMEM((4 * blk, n), bf16)] * 2
    ins = (top, bottom, rtop, rbottom, x, up, down, sc, *ax)
    return call(body, ins, [(x.shape, f32)] * 2, 36 * blk * blk * n, scratch)


def update(mid, rup, rdown, x, sc):
    blk, n = rup.shape

    def body(mid, rup, rdown, x, sc, o):
        step, h = sc[0], sc[1]
        lo, hi = slice(0, blk), slice(blk, 2 * blk)
        for s, r in ((lo, rup), (hi, rdown)):
            o[s, :] = soft(x[s, :] - step * (mid[s, :] + r[...]), h)

    return call(body, (mid, rup, rdown, x, sc), [(x.shape, f32)], 1 << 20)[0]


def per_device(x, observed, fx, bx, fy, by, step_size, threshold):
    blk = fx.shape[2]
    rows, cols = lax.axis_size("row"), lax.axis_size("col")
    downward = [(i, i + 1) for i in range(rows - 1)]
    upward = [(i + 1, i) for i in range(rows - 1)]
    pairs = []
    for first in (0, 1):
        forth = [(i, i + 1) for i in range(first, cols - 1, 2)]
        pairs.append(forth + [(j, i) for i, j in forth])

    def row_swap(to_up, to_down):
        from_up = lax.ppermute(to_down, "row", downward)
        from_down = lax.ppermute(to_up, "row", upward)
        return from_up, from_down

    def chip_swap(a):
        return lax.ppermute(a, "col", pairs[0])

    def col_swap(b):
        return lax.ppermute(b, "col", pairs[1])

    half = cols // 2
    first_hop = [p for p in pairs[1] if set(p) != {half - 1, half}] + [(half - 1, 0), (half, cols - 1)]
    second_hop = [(0, half), (cols - 1, half - 1)]

    def columns(u, fb, merged):
        ua = chip_swap(u)
        ub = col_swap(u)
        if merged:
            w, v = near_misfit(u, ua, observed, byt, fb, 31 * blk // 16)
        else:
            pad = jnp.zeros((16, blk), f32)
            w, v = near_misfit(u, ua, observed, byt, pad, blk + 8)
        vb = lax.ppermute(v, "col", first_hop)
        wb = col_swap(w)
        relayed = lax.ppermute(vb, "col", second_hop)
        qa, qa2, q = full_misfit(w, v, ub, byt, byf)
        ra, ra2 = chip_swap(qa), chip_swap(qa2)
        return back(q, ra, ra2, wb, vb, relayed, u, fb, atx, pos, merged)

    pos = jnp.stack([lax.axis_index("row"), rows, lax.axis_index("col"), cols]).astype(jnp.int32)
    sc = jnp.concatenate([step_size, threshold])
    up, down = row_swap(x[:blk], x[blk:])
    ax, atx, byf, byt, fb = prepare(fx, bx, fy, by, pos)
    u = apply_left(x, up, down, ax)
    top, bottom, *fb = columns(u, fb, True)
    rtop, rbottom = row_swap(top, bottom)
    x, u = update_left(top, bottom, rtop, rbottom, x, up, down, sc, ax)
    top, mid, bottom = columns(u, fb, False)
    rup, rdown = row_swap(top, bottom)
    return update(mid, rup, rdown, x, sc)


def solution(mesh):
    in_specs = (
        P("row", "col"),
        P("row", "col"),
        P("row", None, None, None),
        P("row", None),
        P("col", None, None, None),
        P("col", None),
        P(),
        P(),
    )
    return jax.shard_map(
        per_device, mesh=mesh, in_specs=in_specs, out_specs=P("row", "col"), check_vma=False
    )
```

```python
import jax
import jax.numpy as jnp
from jax import lax
from jax.experimental import pallas as pl
from jax.experimental.pallas import tpu as pltpu
from jax.sharding import PartitionSpec as P

f32 = jnp.float32
bf16 = jnp.bfloat16
VMEM = pl.BlockSpec(memory_space=pltpu.VMEM)
SMEM = pl.BlockSpec(memory_space=pltpu.SMEM)
CHUNK = 256
PAD = 8


def split(x):
    hi = x.astype(bf16)
    return hi, (x - hi.astype(f32)).astype(bf16)


def dot3(xh, xl, yh, yl):
    mm = lambda a, b: jnp.dot(a, b, preferred_element_type=f32)
    return mm(xh, yh) + (mm(xh, yl) + mm(xl, yh))


def soft(v, h):
    return v - jnp.minimum(jnp.maximum(v, -h), h)


def call(body, ins, outs, flops, scratch=(), limit=24 << 20, whole=()):
    size = lambda a: a.size * a.dtype.itemsize
    spec = lambda a: pl.BlockSpec(memory_space=pltpu.HBM) if any(a is w for w in whole) else VMEM
    return pl.pallas_call(
        body,
        out_shape=[jax.ShapeDtypeStruct(s, d) for s, d in outs],
        in_specs=[SMEM if a.size < 64 else spec(a) for a in ins],
        out_specs=[VMEM for _ in outs],
        scratch_shapes=list(scratch),
        compiler_params=pltpu.CompilerParams(vmem_limit_bytes=limit),
        cost_estimate=pl.CostEstimate(
            flops=flops, bytes_accessed=sum(size(a) for a in ins), transcendentals=0
        ),
    )(*ins)


def prepare(fx, fy, pos):
    blk = fx.shape[2]

    def body(fx_hbm, fy_hbm, pos, axh, axl, atxh, atxl, byh, byl, byth, bytl, fb, fx, fy, sem):
        copies = [
            pltpu.make_async_copy(fy_hbm, fy, sem.at[0]),
            pltpu.make_async_copy(fx_hbm, fx, sem.at[1]),
        ]
        for c in copies:
            c.start()
        row, rows, col, cols = pos[0], pos[1], pos[2], pos[3]

        def put(v, k, plain, trans):
            s = slice(k * blk, (k + 1) * blk)
            plain[0][:, s], plain[1][:, s] = split(v)
            trans[0][s, :], trans[1][s, :] = split(v.T)

        copies[0].wait()
        first = jnp.where(col % 2 == 0, 2, 0)
        for k, s in enumerate((first, 1, 2 - first)):
            m = pos[10 + s].astype(f32)
            m = jnp.where((s == 0) & (col == 0), 0.0, m)
            m = jnp.where((s == 2) & (col == cols - 1), 0.0, m)
            v = fy[0, s] * m
            put(v, k, (byh, byl), (byth, bytl))
        fb[:blk, :] = v
        fb[blk:, :] = jnp.zeros((fb.shape[0] - blk, blk), f32)
        copies[1].wait()
        for r in range(2):
            for s in range(3):
                m = pos[4 + 3 * r + s].astype(f32)
                if (r, s) == (0, 0):
                    m = jnp.where(row == 0, 0.0, m)
                if (r, s) == (1, 2):
                    m = jnp.where(row == rows - 1, 0.0, m)
                put(fx[r, s] * m, s, (axh.at[r], axl.at[r]), (atxh.at[r], atxl.at[r]))

    outs = [((2, blk, 3 * blk), bf16)] * 2 + [((2, 3 * blk, blk), bf16)] * 2
    outs += [((blk, 3 * blk), bf16)] * 2 + [((3 * blk, blk), bf16)] * 2
    outs += [((2 * blk + 8, blk), f32)]
    scratch = [pltpu.VMEM(fx.shape, f32), pltpu.VMEM(fy.shape, f32), pltpu.SemaphoreType.DMA((2,))]
    o = call(body, (fx, fy, pos), outs, 1 << 24, scratch, whole=(fx, fy))
    return o[0:2], o[2:4], o[4:6], o[6:8], o[8]


def left(ax, xs, u):
    blk = xs[0].shape[0] // 4
    for r in range(2):
        s = slice(r * blk, (r + 3) * blk)
        u[r * blk : (r + 1) * blk, :] = dot3(ax[0][r], ax[1][r], xs[0][s, :], xs[1][s, :])


def apply_left(x, up, down, ax):
    blk, n = up.shape

    def body(x, up, down, axh, axl, u, xh, xl):
        for t, v in enumerate((up[...], x[:blk, :], x[blk:, :], down[...])):
            s = slice(t * blk, (t + 1) * blk)
            xh[s, :], xl[s, :] = split(v)
        left((axh, axl), (xh, xl), u)

    scratch = [pltpu.VMEM((4 * blk, n), bf16)] * 2
    return call(body, (x, up, down, *ax), [(x.shape, f32)], 36 * blk * blk * n, scratch)[0]


def rows_of(first, second, r):
    cut, (a, b) = first.shape[0], r
    parts = []
    if a < cut:
        parts.append(first[a : min(b, cut), :])
    if b > cut:
        parts.append(second[max(a - cut, 0) : b - cut, :])
    return parts[0] if len(parts) == 1 else jnp.concatenate(parts, axis=0)


def near_misfit(u, ua, observed, byt, cut, fb=None):
    m, blk = u.shape
    ins = (u, ua, observed, *byt) + (() if fb is None else (fb,))

    def body(u, ua, obs, byth, bytl, *rest):
        if fb is not None:
            g, *rest = rest
            g = g[:blk, :]
            rest[2][...], rest[3][...] = split(g)
            rest[4][...], rest[5][...] = split(g.T)
        w, v = rest[:2]
        v[m - cut :, :] = jnp.zeros((PAD + cut - m // 2, blk), f32)
        for i in range(0, m, CHUNK):
            r = slice(i, i + CHUNK)
            acc = -obs[r, :]
            for k, x in enumerate((ua, u)):
                s = slice(k * blk, (k + 1) * blk)
                acc = acc + dot3(*split(x[r, :]), byth[s, :], bytl[s, :])
            here = min(max(cut - i, 0), CHUNK)
            if here:
                w[i : i + here, :] = acc[:here]
            if here < CHUNK:
                v[i + here - cut : i + CHUNK - cut, :] = acc[here:]

    outs = [((cut, blk), f32), ((m // 2 + PAD, blk), f32)]
    outs += [] if fb is None else [((blk, blk), bf16)] * 4
    return call(body, ins, outs, 24 * m * blk * blk)


def full_misfit(w, v, ub, byt, by):
    m, blk = ub.shape

    def body(w, v, ub, byth, bytl, byh, byl, qa, qa2, q):
        b = slice(2 * blk, 3 * blk)
        for i, qa in ((0, qa), (m // 2, qa2)):
            r = slice(i, i + m // 2)
            acc = rows_of(w, v, (i, i + m // 2)) + dot3(*split(ub[r, :]), byth[b, :], bytl[b, :])
            mh, ml = split(acc)
            qa[...] = dot3(mh, ml, byh[:, :blk], byl[:, :blk])
            q[r, :] = dot3(mh, ml, byh[:, blk : 2 * blk], byl[:, blk : 2 * blk])

    outs = [((m // 2, blk), f32)] * 2 + [((m, blk), f32)]
    return call(body, (w, v, ub, *byt, *by), outs, 36 * m * blk * blk)


def back(q, ra, ra2, wb, vb, relayed, u, fb, atx, pos, merged):
    m, n = q.shape
    blk = m // 2
    ins = (q, ra, ra2, wb, vb, relayed, u, *fb, *atx, pos)

    def body(q, ra, ra2, wb, vb, relayed, u, *rest):
        gh, gl, th, tl, ah, al, pos, *outs = rest
        half = pos[3] // 2
        special = (pos[2] == half - 1) | (pos[2] == half) | (pos[2] == 0) | (pos[2] == pos[3] - 1)
        tail = jnp.where(special, relayed[...], vb[...])
        block, flipped = (gh[...], gl[...]), (th[...], tl[...])
        p = []
        for r, a in ((0, ra), (1, ra2)):
            s = slice(r * blk, (r + 1) * blk)
            other = rows_of(wb, tail, (r * blk, (r + 1) * blk)) + dot3(*split(u[s, :]), *flipped)
            v = q[s, :] + a[...] + dot3(*split(other), *block)
            p.append(dot3(ah[r], al[r], *split(v)))
        p0 = p[0][:blk]
        p1 = p[0][blk : 2 * blk] + p[1][:blk]
        p2 = p[0][2 * blk :] + p[1][blk : 2 * blk]
        p3 = p[1][2 * blk :]
        if merged:
            top, bottom = outs
            top[:blk, :], top[blk:, :] = p0, p1
            bottom[:blk, :], bottom[blk:, :] = p2, p3
        else:
            top, mid, bottom = outs
            top[...], bottom[...] = p0, p3
            mid[:blk, :], mid[blk:, :] = p1, p2

    if merged:
        outs = [((m, n), f32)] * 2
    else:
        outs = [((blk, n), f32), ((m, n), f32), ((blk, n), f32)]
    return call(body, ins, outs, 60 * blk * blk * n)


def update_left(top, bottom, rtop, rbottom, x, up, down, sc, ax):
    blk, n = up.shape

    def body(top, bottom, rtop, rbottom, x, up, down, sc, axh, axl, xn, u, xh, xl):
        step, h = sc[0], sc[1]
        lo, hi = slice(0, blk), slice(blk, 2 * blk)
        parts = ((up[...], top, rtop, lo), (x[lo, :], top, rtop, hi))
        parts += ((x[hi, :], bottom, rbottom, lo), (down[...], bottom, rbottom, hi))
        for t, (v, a, b, s) in enumerate(parts):
            new = soft(v - step * (a[s, :] + b[s, :]), h)
            if t in (1, 2):
                xn[(t - 1) * blk : t * blk, :] = new
            d = slice(t * blk, (t + 1) * blk)
            xh[d, :], xl[d, :] = split(new)
        left((axh, axl), (xh, xl), u)

    scratch = [pltpu.VMEM((4 * blk, n), bf16)] * 2
    ins = (top, bottom, rtop, rbottom, x, up, down, sc, *ax)
    return call(body, ins, [(x.shape, f32)] * 2, 36 * blk * blk * n, scratch)


def update(mid, rup, rdown, x, sc):
    blk, n = rup.shape

    def body(mid, rup, rdown, x, sc, o):
        step, h = sc[0], sc[1]
        lo, hi = slice(0, blk), slice(blk, 2 * blk)
        for s, r in ((lo, rup), (hi, rdown)):
            o[s, :] = soft(x[s, :] - step * (mid[s, :] + r[...]), h)

    return call(body, (mid, rup, rdown, x, sc), [(x.shape, f32)], 1 << 20)[0]


def per_device(x, observed, fx, bx, fy, by, step_size, threshold):
    blk = fx.shape[2]
    rows, cols = lax.axis_size("row"), lax.axis_size("col")
    downward = [(i, i + 1) for i in range(rows - 1)]
    upward = [(i + 1, i) for i in range(rows - 1)]
    pairs = []
    for first in (0, 1):
        forth = [(i, i + 1) for i in range(first, cols - 1, 2)]
        pairs.append(forth + [(j, i) for i, j in forth])

    def row_swap(to_up, to_down):
        from_up = lax.ppermute(to_down, "row", downward)
        from_down = lax.ppermute(to_up, "row", upward)
        return from_up, from_down

    def chip_swap(a):
        return lax.ppermute(a, "col", pairs[0])

    def col_swap(b):
        return lax.ppermute(b, "col", pairs[1])

    half = cols // 2
    first_hop = [p for p in pairs[1] if set(p) != {half - 1, half}] + [(half - 1, 0), (half, cols - 1)]
    second_hop = [(0, half), (cols - 1, half - 1)]

    def columns(u, fb, merged):
        ua = chip_swap(u)
        ub = col_swap(u)
        cut = blk + PAD
        if merged:
            w, v, *fb = near_misfit(u, ua, observed, byt, cut, fb)
        else:
            w, v = near_misfit(u, ua, observed, byt, cut)
        vb = lax.ppermute(v, "col", first_hop)
        wb = col_swap(w)
        relayed = lax.ppermute(vb, "col", second_hop)
        qa, qa2, q = full_misfit(w, v, ub, byt, byf)
        ra, ra2 = chip_swap(qa), chip_swap(qa2)
        return (*back(q, ra, ra2, wb, vb, relayed, u, fb, atx, pos, merged), fb)

    pos = jnp.stack([lax.axis_index("row"), rows, lax.axis_index("col"), cols]).astype(jnp.int32)
    pos = jnp.concatenate([pos, bx.reshape(-1), by.reshape(-1)])
    sc = jnp.concatenate([step_size, threshold])
    up, down = row_swap(x[:blk], x[blk:])
    ax, atx, byf, byt, fb = prepare(fx, fy, pos)
    u = apply_left(x, up, down, ax)
    top, bottom, fb = columns(u, col_swap(fb), True)
    rtop, rbottom = row_swap(top, bottom)
    x, u = update_left(top, bottom, rtop, rbottom, x, up, down, sc, ax)
    top, mid, bottom, _ = columns(u, fb, False)
    rup, rdown = row_swap(top, bottom)
    return update(mid, rup, rdown, x, sc)


def solution(mesh):
    in_specs = (
        P("row", "col"),
        P("row", "col"),
        P("row", None, None, None),
        P("row", None),
        P("col", None, None, None),
        P("col", None),
        P(),
        P(),
    )
    return jax.shard_map(
        per_device, mesh=mesh, in_specs=in_specs, out_specs=P("row", "col"), check_vma=False
    )
```

```python
import jax
import jax.numpy as jnp
from jax import lax
from jax.experimental import pallas as pl
from jax.experimental.pallas import tpu as pltpu
from jax.sharding import PartitionSpec as P

f32 = jnp.float32
bf16 = jnp.bfloat16
VMEM = pl.BlockSpec(memory_space=pltpu.VMEM)
SMEM = pl.BlockSpec(memory_space=pltpu.SMEM)
CHUNK = 256
PAD = 8


def split(x):
    hi = x.astype(bf16)
    return hi, (x - hi.astype(f32)).astype(bf16)


def dot3(xh, xl, yh, yl):
    mm = lambda a, b: jnp.dot(a, b, preferred_element_type=f32)
    return mm(xh, yh) + (mm(xh, yl) + mm(xl, yh))


def soft(v, h):
    return v - jnp.minimum(jnp.maximum(v, -h), h)


def call(body, ins, outs, flops, scratch=(), limit=24 << 20, whole=()):
    size = lambda a: a.size * a.dtype.itemsize
    spec = lambda a: pl.BlockSpec(memory_space=pltpu.HBM) if any(a is w for w in whole) else VMEM
    return pl.pallas_call(
        body,
        out_shape=[jax.ShapeDtypeStruct(s, d) for s, d in outs],
        in_specs=[SMEM if a.size < 64 else spec(a) for a in ins],
        out_specs=[VMEM for _ in outs],
        scratch_shapes=list(scratch),
        compiler_params=pltpu.CompilerParams(vmem_limit_bytes=limit),
        cost_estimate=pl.CostEstimate(
            flops=flops, bytes_accessed=sum(size(a) for a in ins), transcendentals=0
        ),
    )(*ins)


def prepare(fx, fy, pos):
    blk = fx.shape[2]

    def body(fx_hbm, fy_hbm, pos, axh, axl, atxh, atxl, byh, byl, byth, bytl, fb, fx, fy, sem):
        copies = [
            pltpu.make_async_copy(fy_hbm, fy, sem.at[0]),
            pltpu.make_async_copy(fx_hbm, fx, sem.at[1]),
        ]
        for c in copies:
            c.start()
        row, rows, col, cols = pos[0], pos[1], pos[2], pos[3]

        def put(v, k, plain, trans):
            s = slice(k * blk, (k + 1) * blk)
            plain[0][:, s], plain[1][:, s] = split(v)
            trans[0][s, :], trans[1][s, :] = split(v.T)

        copies[0].wait()
        first = jnp.where(col % 2 == 0, 2, 0)
        for k, s in enumerate((first, 1, 2 - first)):
            m = pos[10 + s].astype(f32)
            m = jnp.where((s == 0) & (col == 0), 0.0, m)
            m = jnp.where((s == 2) & (col == cols - 1), 0.0, m)
            v = fy[0, s] * m
            put(v, k, (byh, byl), (byth, bytl))
        fb[:blk, :] = v
        fb[blk:, :] = jnp.zeros((fb.shape[0] - blk, blk), f32)
        copies[1].wait()
        for r in range(2):
            for s in range(3):
                m = pos[4 + 3 * r + s].astype(f32)
                if (r, s) == (0, 0):
                    m = jnp.where(row == 0, 0.0, m)
                if (r, s) == (1, 2):
                    m = jnp.where(row == rows - 1, 0.0, m)
                put(fx[r, s] * m, s, (axh.at[r], axl.at[r]), (atxh.at[r], atxl.at[r]))

    outs = [((2, blk, 3 * blk), bf16)] * 2 + [((2, 3 * blk, blk), bf16)] * 2
    outs += [((blk, 3 * blk), bf16)] * 2 + [((3 * blk, blk), bf16)] * 2
    outs += [((2 * blk + 8, blk), f32)]
    scratch = [pltpu.VMEM(fx.shape, f32), pltpu.VMEM(fy.shape, f32), pltpu.SemaphoreType.DMA((2,))]
    o = call(body, (fx, fy, pos), outs, 1 << 24, scratch, whole=(fx, fy))
    return o[0:2], o[2:4], o[4:6], o[6:8], o[8]


def left(ax, xs, u):
    blk = xs[0].shape[0] // 4
    for r in range(2):
        s = slice(r * blk, (r + 3) * blk)
        u[r * blk : (r + 1) * blk, :] = dot3(ax[0][r], ax[1][r], xs[0][s, :], xs[1][s, :])


def apply_left(x, up, down, ax):
    blk, n = up.shape

    def body(x, up, down, axh, axl, u, xh, xl):
        for t, v in enumerate((up[...], x[:blk, :], x[blk:, :], down[...])):
            s = slice(t * blk, (t + 1) * blk)
            xh[s, :], xl[s, :] = split(v)
        left((axh, axl), (xh, xl), u)

    scratch = [pltpu.VMEM((4 * blk, n), bf16)] * 2
    return call(body, (x, up, down, *ax), [(x.shape, f32)], 36 * blk * blk * n, scratch)[0]


def rows_of(first, second, r):
    cut, (a, b) = first.shape[0], r
    parts = []
    if a < cut:
        parts.append(first[a : min(b, cut), :])
    if b > cut:
        parts.append(second[max(a - cut, 0) : b - cut, :])
    return parts[0] if len(parts) == 1 else jnp.concatenate(parts, axis=0)


def near_misfit(u, ua, observed, byt, cut, fb=None):
    m, blk = u.shape
    ins = (u, ua, observed, *byt) + (() if fb is None else (fb,))

    def body(u, ua, obs, byth, bytl, *rest):
        if fb is not None:
            g, *rest = rest
            g = g[:blk, :]
            rest[2][...], rest[3][...] = split(g)
            rest[4][...], rest[5][...] = split(g.T)
        w, v = rest[:2]
        v[m - cut :, :] = jnp.zeros((PAD + cut - m // 2, blk), f32)
        for i in range(0, m, CHUNK):
            r = slice(i, i + CHUNK)
            acc = -obs[r, :]
            for k, x in enumerate((ua, u)):
                s = slice(k * blk, (k + 1) * blk)
                acc = acc + dot3(*split(x[r, :]), byth[s, :], bytl[s, :])
            here = min(max(cut - i, 0), CHUNK)
            if here:
                w[i : i + here, :] = acc[:here]
            if here < CHUNK:
                v[i + here - cut : i + CHUNK - cut, :] = acc[here:]

    outs = [((cut, blk), f32), ((m // 2 + PAD, blk), f32)]
    outs += [] if fb is None else [((blk, blk), bf16)] * 4
    return call(body, ins, outs, 24 * m * blk * blk)


def full_misfit(w, v, ub, byt, by):
    m, blk = ub.shape

    def body(w, v, ub, byth, bytl, byh, byl, qa, qa2, q):
        b = slice(2 * blk, 3 * blk)
        for i, qa in ((0, qa), (m // 2, qa2)):
            r = slice(i, i + m // 2)
            acc = rows_of(w, v, (i, i + m // 2)) + dot3(*split(ub[r, :]), byth[b, :], bytl[b, :])
            mh, ml = split(acc)
            qa[...] = dot3(mh, ml, byh[:, :blk], byl[:, :blk])
            q[r, :] = dot3(mh, ml, byh[:, blk : 2 * blk], byl[:, blk : 2 * blk])

    outs = [((m // 2, blk), f32)] * 2 + [((m, blk), f32)]
    return call(body, (w, v, ub, *byt, *by), outs, 36 * m * blk * blk)


def back(q, ra, ra2, wb, vb, relayed, u, fb, atx, pos, merged):
    m, n = q.shape
    blk = m // 2
    ins = (q, ra, ra2, wb, vb, relayed, u, *fb, *atx, pos)

    def body(q, ra, ra2, wb, vb, relayed, u, *rest):
        gh, gl, th, tl, ah, al, pos, *outs = rest
        half = pos[3] // 2
        special = (pos[2] == half - 1) | (pos[2] == half) | (pos[2] == 0) | (pos[2] == pos[3] - 1)
        tail = jnp.where(special, relayed[...], vb[...])
        block, flipped = (gh[...], gl[...]), (th[...], tl[...])
        p = []
        for r, a in ((0, ra), (1, ra2)):
            s = slice(r * blk, (r + 1) * blk)
            other = rows_of(wb, tail, (r * blk, (r + 1) * blk)) + dot3(*split(u[s, :]), *flipped)
            v = q[s, :] + a[...] + dot3(*split(other), *block)
            p.append(dot3(ah[r], al[r], *split(v)))
        p0 = p[0][:blk]
        p1 = p[0][blk : 2 * blk] + p[1][:blk]
        p2 = p[0][2 * blk :] + p[1][blk : 2 * blk]
        p3 = p[1][2 * blk :]
        if merged:
            top, bottom = outs
            top[:blk, :], top[blk:m, :] = p0, p1
            top[m:, :] = jnp.zeros((PAD, n), f32)
            bottom[:blk, :], bottom[blk:, :] = p2, p3
        else:
            top, mid, bottom = outs
            top[...], bottom[...] = p0, p3
            mid[:blk, :], mid[blk:, :] = p1, p2

    if merged:
        outs = [((m + PAD, n), f32), ((m, n), f32)]
    else:
        outs = [((blk, n), f32), ((m, n), f32), ((blk, n), f32)]
    return call(body, ins, outs, 60 * blk * blk * n)


def update_left(top, bottom, rtop, rbottom, x, up, down, sc, ax):
    blk, n = up.shape

    def body(top, bottom, rtop, rbottom, x, up, down, sc, axh, axl, xn, u, xh, xl):
        step, h = sc[0], sc[1]
        lo, hi = slice(0, blk), slice(blk, 2 * blk)
        parts = ((up[...], top, rtop, lo), (x[lo, :], top, rtop, hi))
        parts += ((x[hi, :], bottom, rbottom, lo), (down[...], bottom, rbottom, hi))
        for t, (v, a, b, s) in enumerate(parts):
            new = soft(v - step * (a[s, :] + b[s, :]), h)
            if t in (1, 2):
                xn[(t - 1) * blk : t * blk, :] = new
            d = slice(t * blk, (t + 1) * blk)
            xh[d, :], xl[d, :] = split(new)
        left((axh, axl), (xh, xl), u)

    scratch = [pltpu.VMEM((4 * blk, n), bf16)] * 2
    ins = (top, bottom, rtop, rbottom, x, up, down, sc, *ax)
    return call(body, ins, [(x.shape, f32)] * 2, 36 * blk * blk * n, scratch)


def update(mid, rup, rdown, x, sc):
    blk, n = rup.shape

    def body(mid, rup, rdown, x, sc, o):
        step, h = sc[0], sc[1]
        lo, hi = slice(0, blk), slice(blk, 2 * blk)
        for s, r in ((lo, rup), (hi, rdown)):
            o[s, :] = soft(x[s, :] - step * (mid[s, :] + r[...]), h)

    return call(body, (mid, rup, rdown, x, sc), [(x.shape, f32)], 1 << 20)[0]


def per_device(x, observed, fx, bx, fy, by, step_size, threshold):
    blk = fx.shape[2]
    rows, cols = lax.axis_size("row"), lax.axis_size("col")
    downward = [(i, i + 1) for i in range(rows - 1)]
    upward = [(i + 1, i) for i in range(rows - 1)]
    pairs = []
    for first in (0, 1):
        forth = [(i, i + 1) for i in range(first, cols - 1, 2)]
        pairs.append(forth + [(j, i) for i, j in forth])

    def row_swap(to_up, to_down):
        from_up = lax.ppermute(to_down, "row", downward)
        from_down = lax.ppermute(to_up, "row", upward)
        return from_up, from_down

    def chip_swap(a):
        return lax.ppermute(a, "col", pairs[0])

    def col_swap(b):
        return lax.ppermute(b, "col", pairs[1])

    half = cols // 2
    first_hop = [p for p in pairs[1] if set(p) != {half - 1, half}] + [(half - 1, 0), (half, cols - 1)]
    second_hop = [(0, half), (cols - 1, half - 1)]

    def columns(u, fb, merged):
        ua = chip_swap(u)
        ub = col_swap(u)
        cut = blk + PAD
        if merged:
            w, v, *fb = near_misfit(u, ua, observed, byt, cut, fb)
        else:
            w, v = near_misfit(u, ua, observed, byt, cut)
        vb = lax.ppermute(v, "col", first_hop)
        wb = col_swap(w)
        relayed = lax.ppermute(vb, "col", second_hop)
        qa, qa2, q = full_misfit(w, v, ub, byt, byf)
        ra, ra2 = chip_swap(qa), chip_swap(qa2)
        return (*back(q, ra, ra2, wb, vb, relayed, u, fb, atx, pos, merged), fb)

    pos = jnp.stack([lax.axis_index("row"), rows, lax.axis_index("col"), cols]).astype(jnp.int32)
    pos = jnp.concatenate([pos, bx.reshape(-1), by.reshape(-1)])
    sc = jnp.concatenate([step_size, threshold])
    up, down = row_swap(x[:blk], x[blk:])
    ax, atx, byf, byt, fb = prepare(fx, fy, pos)
    u = apply_left(x, up, down, ax)
    top, bottom, fb = columns(u, col_swap(fb), True)
    rtop, rbottom = row_swap(top, bottom)
    x, u = update_left(top, bottom, rtop, rbottom, x, up, down, sc, ax)
    top, mid, bottom, _ = columns(u, fb, False)
    rup, rdown = row_swap(top, bottom)
    return update(mid, rup, rdown, x, sc)


def solution(mesh):
    in_specs = (
        P("row", "col"),
        P("row", "col"),
        P("row", None, None, None),
        P("row", None),
        P("col", None, None, None),
        P("col", None),
        P(),
        P(),
    )
    return jax.shard_map(
        per_device, mesh=mesh, in_specs=in_specs, out_specs=P("row", "col"), check_vma=False
    )
```

```python
import jax
import jax.numpy as jnp
from jax import lax
from jax.experimental import pallas as pl
from jax.experimental.pallas import tpu as pltpu
from jax.sharding import PartitionSpec as P

f32 = jnp.float32
bf16 = jnp.bfloat16
VMEM = pl.BlockSpec(memory_space=pltpu.VMEM)
SMEM = pl.BlockSpec(memory_space=pltpu.SMEM)
CHUNK = 256
PAD = 8


def split(x):
    hi = x.astype(bf16)
    return hi, (x - hi.astype(f32)).astype(bf16)


def dot3(xh, xl, yh, yl):
    mm = lambda a, b: jnp.dot(a, b, preferred_element_type=f32)
    return mm(xh, yh) + (mm(xh, yl) + mm(xl, yh))


def soft(v, h):
    return v - jnp.minimum(jnp.maximum(v, -h), h)


def call(body, ins, outs, flops, scratch=(), limit=24 << 20, whole=()):
    size = lambda a: a.size * a.dtype.itemsize
    spec = lambda a: pl.BlockSpec(memory_space=pltpu.HBM) if any(a is w for w in whole) else VMEM
    return pl.pallas_call(
        body,
        out_shape=[jax.ShapeDtypeStruct(s, d) for s, d in outs],
        in_specs=[SMEM if a.size < 64 else spec(a) for a in ins],
        out_specs=[VMEM for _ in outs],
        scratch_shapes=list(scratch),
        compiler_params=pltpu.CompilerParams(vmem_limit_bytes=limit),
        cost_estimate=pl.CostEstimate(
            flops=flops, bytes_accessed=sum(size(a) for a in ins), transcendentals=0
        ),
    )(*ins)


def prepare(fx, fy, pos):
    blk = fx.shape[2]

    def body(fx_hbm, fy_hbm, pos, axh, axl, atxh, atxl, byh, byl, byth, bytl, fb, fx, fy, sem):
        copies = [
            pltpu.make_async_copy(fy_hbm, fy, sem.at[0]),
            pltpu.make_async_copy(fx_hbm, fx, sem.at[1]),
        ]
        for c in copies:
            c.start()
        row, rows, col, cols = pos[0], pos[1], pos[2], pos[3]

        def put(v, k, plain, trans):
            s = slice(k * blk, (k + 1) * blk)
            plain[0][:, s], plain[1][:, s] = split(v)
            trans[0][s, :], trans[1][s, :] = split(v.T)

        copies[0].wait()
        first = jnp.where(col % 2 == 0, 2, 0)
        for k, s in enumerate((first, 1, 2 - first)):
            m = pos[10 + s].astype(f32)
            m = jnp.where((s == 0) & (col == 0), 0.0, m)
            m = jnp.where((s == 2) & (col == cols - 1), 0.0, m)
            v = fy[0, s] * m
            put(v, k, (byh, byl), (byth, bytl))
        fb[:blk, :] = v
        fb[blk:, :] = jnp.zeros((fb.shape[0] - blk, blk), f32)
        copies[1].wait()
        for r in range(2):
            for s in range(3):
                m = pos[4 + 3 * r + s].astype(f32)
                if (r, s) == (0, 0):
                    m = jnp.where(row == 0, 0.0, m)
                if (r, s) == (1, 2):
                    m = jnp.where(row == rows - 1, 0.0, m)
                put(fx[r, s] * m, s, (axh.at[r], axl.at[r]), (atxh.at[r], atxl.at[r]))

    outs = [((2, blk, 3 * blk), bf16)] * 2 + [((2, 3 * blk, blk), bf16)] * 2
    outs += [((blk, 3 * blk), bf16)] * 2 + [((3 * blk, blk), bf16)] * 2
    outs += [((blk + PAD, blk), f32)]
    scratch = [pltpu.VMEM(fx.shape, f32), pltpu.VMEM(fy.shape, f32), pltpu.SemaphoreType.DMA((2,))]
    o = call(body, (fx, fy, pos), outs, 1 << 24, scratch, whole=(fx, fy))
    return o[0:2], o[2:4], o[4:6], o[6:8], o[8]


def left(ax, xs, u):
    blk = xs[0].shape[0] // 4
    for r in range(2):
        s = slice(r * blk, (r + 3) * blk)
        u[r * blk : (r + 1) * blk, :] = dot3(ax[0][r], ax[1][r], xs[0][s, :], xs[1][s, :])


def apply_left(x, up, down, ax):
    blk, n = up.shape

    def body(x, up, down, axh, axl, u, first, second, xh, xl):
        for t, v in enumerate((up[...], x[:blk, :], x[blk:, :], down[...])):
            s = slice(t * blk, (t + 1) * blk)
            xh[s, :], xl[s, :] = split(v)
        left((axh, axl), (xh, xl), u)
        first[...], second[...] = u[:blk, :], u[blk:, :]

    scratch = [pltpu.VMEM((4 * blk, n), bf16)] * 2
    outs = [(x.shape, f32)] + [(up.shape, f32)] * 2
    return call(body, (x, up, down, *ax), outs, 36 * blk * blk * n, scratch)


def rows_of(first, second, r):
    cut, (a, b) = first.shape[0], r
    parts = []
    if a < cut:
        parts.append(first[a : min(b, cut), :])
    if b > cut:
        parts.append(second[max(a - cut, 0) : b - cut, :])
    return parts[0] if len(parts) == 1 else jnp.concatenate(parts, axis=0)


def near_misfit(u, parts, observed, byt, cut, fb=None):
    m, blk = u.shape
    ins = (u, observed, *byt, *parts) + (() if fb is None else (fb,))

    def body(u, obs, byth, bytl, *rest):
        uas, rest = rest[: len(parts)], rest[len(parts) :]
        rows = m // len(parts)
        if fb is not None:
            g, *rest = rest
            g = g[:blk, :]
            rest[2][...], rest[3][...] = split(g)
            rest[4][...], rest[5][...] = split(g.T)
        w, v = rest[:2]
        v[m - cut :, :] = jnp.zeros((PAD + cut - m // 2, blk), f32)
        for i in range(0, m, CHUNK):
            r = slice(i, i + CHUNK)
            acc = -obs[r, :]
            ua = uas[i // rows][i % rows : i % rows + CHUNK, :]
            for k, x in enumerate((ua, u[r, :])):
                s = slice(k * blk, (k + 1) * blk)
                acc = acc + dot3(*split(x), byth[s, :], bytl[s, :])
            here = min(max(cut - i, 0), CHUNK)
            if here:
                w[i : i + here, :] = acc[:here]
            if here < CHUNK:
                v[i + here - cut : i + CHUNK - cut, :] = acc[here:]

    outs = [((cut, blk), f32), ((m // 2 + PAD, blk), f32)]
    outs += [] if fb is None else [((blk, blk), bf16)] * 4
    return call(body, ins, outs, 24 * m * blk * blk)


def full_misfit(w, v, ub, byt, by):
    m, blk = ub.shape

    def body(w, v, ub, byth, bytl, byh, byl, qa, qa2, q):
        b = slice(2 * blk, 3 * blk)
        for i, qa in ((0, qa), (m // 2, qa2)):
            r = slice(i, i + m // 2)
            acc = rows_of(w, v, (i, i + m // 2)) + dot3(*split(ub[r, :]), byth[b, :], bytl[b, :])
            mh, ml = split(acc)
            qa[...] = dot3(mh, ml, byh[:, :blk], byl[:, :blk])
            q[r, :] = dot3(mh, ml, byh[:, blk : 2 * blk], byl[:, blk : 2 * blk])

    outs = [((m // 2, blk), f32)] * 2 + [((m, blk), f32)]
    return call(body, (w, v, ub, *byt, *by), outs, 36 * m * blk * blk)


def back(q, ra, ra2, wb, vb, relayed, u, fb, atx, pos, merged):
    m, n = q.shape
    blk = m // 2
    ins = (q, ra, ra2, wb, vb, relayed, u, *fb, *atx, pos)

    def body(q, ra, ra2, wb, vb, relayed, u, *rest):
        gh, gl, th, tl, ah, al, pos, *outs = rest
        half = pos[3] // 2
        special = (pos[2] == half - 1) | (pos[2] == half) | (pos[2] == 0) | (pos[2] == pos[3] - 1)
        tail = jnp.where(special, relayed[...], vb[...])
        block, flipped = (gh[...], gl[...]), (th[...], tl[...])
        p = []
        for r, a in ((0, ra), (1, ra2)):
            s = slice(r * blk, (r + 1) * blk)
            other = rows_of(wb, tail, (r * blk, (r + 1) * blk)) + dot3(*split(u[s, :]), *flipped)
            v = q[s, :] + a[...] + dot3(*split(other), *block)
            p.append(dot3(ah[r], al[r], *split(v)))
        p0 = p[0][:blk]
        p1 = p[0][blk : 2 * blk] + p[1][:blk]
        p2 = p[0][2 * blk :] + p[1][blk : 2 * blk]
        p3 = p[1][2 * blk :]
        if merged:
            top, bottom = outs
            top[:blk, :], top[blk:m, :] = p0, p1
            top[m:, :] = jnp.zeros((PAD, n), f32)
            bottom[:blk, :], bottom[blk:, :] = p2, p3
        else:
            top, mid, bottom = outs
            top[...], bottom[...] = p0, p3
            mid[:blk, :], mid[blk:, :] = p1, p2

    if merged:
        outs = [((m + PAD, n), f32), ((m, n), f32)]
    else:
        outs = [((blk, n), f32), ((m, n), f32), ((blk, n), f32)]
    return call(body, ins, outs, 60 * blk * blk * n)


def update_left(top, bottom, rtop, rbottom, x, up, down, sc, ax):
    blk, n = up.shape

    def body(top, bottom, rtop, rbottom, x, up, down, sc, axh, axl, xn, u, xh, xl):
        step, h = sc[0], sc[1]
        lo, hi = slice(0, blk), slice(blk, 2 * blk)
        parts = ((up[...], top, rtop, lo), (x[lo, :], top, rtop, hi))
        parts += ((x[hi, :], bottom, rbottom, lo), (down[...], bottom, rbottom, hi))
        for t, (v, a, b, s) in enumerate(parts):
            new = soft(v - step * (a[s, :] + b[s, :]), h)
            if t in (1, 2):
                xn[(t - 1) * blk : t * blk, :] = new
            d = slice(t * blk, (t + 1) * blk)
            xh[d, :], xl[d, :] = split(new)
        left((axh, axl), (xh, xl), u)

    scratch = [pltpu.VMEM((4 * blk, n), bf16)] * 2
    ins = (top, bottom, rtop, rbottom, x, up, down, sc, *ax)
    return call(body, ins, [(x.shape, f32)] * 2, 36 * blk * blk * n, scratch)


def update(mid, rup, rdown, x, sc):
    blk, n = rup.shape

    def body(mid, rup, rdown, x, sc, o):
        step, h = sc[0], sc[1]
        lo, hi = slice(0, blk), slice(blk, 2 * blk)
        for s, r in ((lo, rup), (hi, rdown)):
            o[s, :] = soft(x[s, :] - step * (mid[s, :] + r[...]), h)

    return call(body, (mid, rup, rdown, x, sc), [(x.shape, f32)], 1 << 20)[0]


def per_device(x, observed, fx, bx, fy, by, step_size, threshold):
    blk = fx.shape[2]
    rows, cols = lax.axis_size("row"), lax.axis_size("col")
    downward = [(i, i + 1) for i in range(rows - 1)]
    upward = [(i + 1, i) for i in range(rows - 1)]
    pairs = []
    for first in (0, 1):
        forth = [(i, i + 1) for i in range(first, cols - 1, 2)]
        pairs.append(forth + [(j, i) for i, j in forth])

    def row_swap(to_up, to_down):
        from_up = lax.ppermute(to_down, "row", downward)
        from_down = lax.ppermute(to_up, "row", upward)
        return from_up, from_down

    def chip_swap(a):
        return lax.ppermute(a, "col", pairs[0])

    def col_swap(b):
        return lax.ppermute(b, "col", pairs[1])

    half = cols // 2
    first_hop = [p for p in pairs[1] if set(p) != {half - 1, half}] + [(half - 1, 0), (half, cols - 1)]
    second_hop = [(0, half), (cols - 1, half - 1)]

    def columns(u, halves, fb, merged):
        ub = col_swap(u)
        cut = blk + PAD
        if merged:
            parts = [chip_swap(v) for v in halves]
            w, v, *fb = near_misfit(u, parts, observed, byt, cut, fb)
        else:
            w, v = near_misfit(u, [chip_swap(u)], observed, byt, cut)
        vb = lax.ppermute(v, "col", first_hop)
        wb = col_swap(w)
        relayed = lax.ppermute(vb, "col", second_hop)
        qa, qa2, q = full_misfit(w, v, ub, byt, byf)
        ra, ra2 = chip_swap(qa), chip_swap(qa2)
        return (*back(q, ra, ra2, wb, vb, relayed, u, fb, atx, pos, merged), fb)

    pos = jnp.stack([lax.axis_index("row"), rows, lax.axis_index("col"), cols]).astype(jnp.int32)
    pos = jnp.concatenate([pos, bx.reshape(-1), by.reshape(-1)])
    sc = jnp.concatenate([step_size, threshold])
    up, down = row_swap(x[:blk], x[blk:])
    ax, atx, byf, byt, fb = prepare(fx, fy, pos)
    u, *halves = apply_left(x, up, down, ax)
    top, bottom, fb = columns(u, halves, col_swap(fb), True)
    rtop, rbottom = row_swap(top, bottom)
    x, u = update_left(top, bottom, rtop, rbottom, x, up, down, sc, ax)
    top, mid, bottom, _ = columns(u, None, fb, False)
    rup, rdown = row_swap(top, bottom)
    return update(mid, rup, rdown, x, sc)


def solution(mesh):
    in_specs = (
        P("row", "col"),
        P("row", "col"),
        P("row", None, None, None),
        P("row", None),
        P("col", None, None, None),
        P("col", None),
        P(),
        P(),
    )
    return jax.shard_map(
        per_device, mesh=mesh, in_specs=in_specs, out_specs=P("row", "col"), check_vma=False
    )
```

```python
import jax
import jax.numpy as jnp
from jax import lax
from jax.experimental import pallas as pl
from jax.experimental.pallas import tpu as pltpu
from jax.sharding import PartitionSpec as P

f32 = jnp.float32
bf16 = jnp.bfloat16
VMEM = pl.BlockSpec(memory_space=pltpu.VMEM)
SMEM = pl.BlockSpec(memory_space=pltpu.SMEM)
CHUNK = 256


def split(x):
    hi = x.astype(bf16)
    return hi, (x - hi.astype(f32)).astype(bf16)


def dot3(xh, xl, yh, yl):
    mm = lambda a, b: jnp.dot(a, b, preferred_element_type=f32)
    return mm(xh, yh) + (mm(xh, yl) + mm(xl, yh))


def soft(v, h):
    return v - jnp.minimum(jnp.maximum(v, -h), h)


def call(body, ins, outs, flops, scratch=(), limit=24 << 20):
    size = lambda a: a.size * a.dtype.itemsize
    return pl.pallas_call(
        body,
        out_shape=[jax.ShapeDtypeStruct(s, d) for s, d in outs],
        in_specs=[SMEM if a.size < 64 else VMEM for a in ins],
        out_specs=[VMEM for _ in outs],
        scratch_shapes=list(scratch),
        compiler_params=pltpu.CompilerParams(vmem_limit_bytes=limit),
        cost_estimate=pl.CostEstimate(
            flops=flops, bytes_accessed=sum(size(a) for a in ins), transcendentals=0
        ),
    )(*ins)


def prepare(fx, bx, fy, by, pos):
    blk = fx.shape[2]

    def body(fx, bx, fy, by, pos, axh, axl, atxh, atxl, byh, byl, byth, bytl, fb):
        row, rows, col, cols = pos[0], pos[1], pos[2], pos[3]

        def put(v, k, plain, trans):
            s = slice(k * blk, (k + 1) * blk)
            plain[0][:, s], plain[1][:, s] = split(v)
            trans[0][s, :], trans[1][s, :] = split(v.T)

        for r in range(2):
            for s in range(3):
                m = bx[r, s].astype(f32)
                if (r, s) == (0, 0):
                    m = jnp.where(row == 0, 0.0, m)
                if (r, s) == (1, 2):
                    m = jnp.where(row == rows - 1, 0.0, m)
                put(fx[r, s] * m, s, (axh.at[r], axl.at[r]), (atxh.at[r], atxl.at[r]))
        first = jnp.where(col % 2 == 0, 2, 0)
        for k, s in enumerate((first, 1, 2 - first)):
            m = by[0, s].astype(f32)
            m = jnp.where((s == 0) & (col == 0), 0.0, m)
            m = jnp.where((s == 2) & (col == cols - 1), 0.0, m)
            v = fy[0, s] * m
            put(v, k, (byh, byl), (byth, bytl))
        fb[...] = v

    outs = [((2, blk, 3 * blk), bf16)] * 2 + [((2, 3 * blk, blk), bf16)] * 2
    outs += [((blk, 3 * blk), bf16)] * 2 + [((3 * blk, blk), bf16)] * 2
    outs += [((blk, blk), f32)]
    o = call(body, (fx, bx, fy, by, pos), outs, 1 << 24)
    return o[0:2], o[2:4], o[4:6], o[6:8], o[8]


def left(ax, xs, u):
    blk = xs[0].shape[0] // 4
    for r in range(2):
        s = slice(r * blk, (r + 3) * blk)
        u[r * blk : (r + 1) * blk, :] = dot3(ax[0][r], ax[1][r], xs[0][s, :], xs[1][s, :])


def apply_left(x, up, down, ax):
    blk, n = up.shape

    def body(x, up, down, axh, axl, u, xh, xl):
        for t, v in enumerate((up[...], x[:blk, :], x[blk:, :], down[...])):
            s = slice(t * blk, (t + 1) * blk)
            xh[s, :], xl[s, :] = split(v)
        left((axh, axl), (xh, xl), u)

    scratch = [pltpu.VMEM((4 * blk, n), bf16)] * 2
    return call(body, (x, up, down, *ax), [(x.shape, f32)], 36 * blk * blk * n, scratch)[0]


def rows_of(first, second, r):
    cut, (a, b) = first.shape[0], r
    parts = []
    if a < cut:
        parts.append(first[a : min(b, cut), :])
    if b > cut:
        parts.append(second[max(a - cut, 0) : b - cut, :])
    return parts[0] if len(parts) == 1 else jnp.concatenate(parts, axis=0)


def near_misfit(u, ua, observed, byt, below, cut):
    m, blk = u.shape
    extra = below.shape[0]

    def body(u, ua, obs, byth, bytl, below, w, v):
        v[m - cut :, :] = below[...]
        for i in range(0, m, CHUNK):
            r = slice(i, i + CHUNK)
            acc = -obs[r, :]
            for k, x in enumerate((ua, u)):
                s = slice(k * blk, (k + 1) * blk)
                acc = acc + dot3(*split(x[r, :]), byth[s, :], bytl[s, :])
            here = min(max(cut - i, 0), CHUNK)
            if here:
                w[i : i + here, :] = acc[:here]
            if here < CHUNK:
                v[i + here - cut : i + CHUNK - cut, :] = acc[here:]

    outs = [((cut, blk), f32), ((m - cut + extra, blk), f32)]
    return call(body, (u, ua, observed, *byt, below), outs, 24 * m * blk * blk)


def full_misfit(w, v, ub, byt, by):
    m, blk = ub.shape

    def body(w, v, ub, byth, bytl, byh, byl, qa, qa2, q):
        b = slice(2 * blk, 3 * blk)
        for i, qa in ((0, qa), (m // 2, qa2)):
            r = slice(i, i + m // 2)
            acc = rows_of(w, v, (i, i + m // 2)) + dot3(*split(ub[r, :]), byth[b, :], bytl[b, :])
            mh, ml = split(acc)
            qa[...] = dot3(mh, ml, byh[:, :blk], byl[:, :blk])
            q[r, :] = dot3(mh, ml, byh[:, blk : 2 * blk], byl[:, blk : 2 * blk])

    outs = [((m // 2, blk), f32)] * 2 + [((m, blk), f32)]
    return call(body, (w, v, ub, *byt, *by), outs, 36 * m * blk * blk)


def back(q, ra, ra2, wb, vb, relayed, u, fb, atx, pos, merged):
    m, n = q.shape
    blk = m // 2
    cut = wb.shape[0]
    ins = (q, ra, ra2, wb, vb, relayed, u, *(() if merged else fb), *atx, pos)

    def body(q, ra, ra2, wb, vb, relayed, u, *rest):
        if merged:
            ah, al, pos, *outs = rest
        else:
            gh, gl, th, tl, ah, al, pos, *outs = rest
        half = pos[3] // 2
        special = (pos[2] == half - 1) | (pos[2] == half) | (pos[2] == 0) | (pos[2] == pos[3] - 1)
        tail = jnp.where(special, relayed[...], vb[...])
        if merged:
            *outs, gh, gl, th, tl = outs
            g = tail[m - cut : m - cut + blk]
            gh[...], gl[...] = split(g)
            th[...], tl[...] = split(g.T)
        block, flipped = (gh[...], gl[...]), (th[...], tl[...])
        p = []
        for r, a in ((0, ra), (1, ra2)):
            s = slice(r * blk, (r + 1) * blk)
            other = rows_of(wb, tail, (r * blk, (r + 1) * blk)) + dot3(*split(u[s, :]), *flipped)
            v = q[s, :] + a[...] + dot3(*split(other), *block)
            p.append(dot3(ah[r], al[r], *split(v)))
        p0 = p[0][:blk]
        p1 = p[0][blk : 2 * blk] + p[1][:blk]
        p2 = p[0][2 * blk :] + p[1][blk : 2 * blk]
        p3 = p[1][2 * blk :]
        if merged:
            top, bottom = outs
            top[:blk, :], top[blk:, :] = p0, p1
            bottom[:blk, :], bottom[blk:, :] = p2, p3
        else:
            top, mid, bottom = outs
            top[...], bottom[...] = p0, p3
            mid[:blk, :], mid[blk:, :] = p1, p2

    if merged:
        outs = [((m, n), f32)] * 2 + [((n, n), bf16)] * 4
    else:
        outs = [((blk, n), f32), ((m, n), f32), ((blk, n), f32)]
    return call(body, ins, outs, 60 * blk * blk * n)


def update_left(top, bottom, rtop, rbottom, x, up, down, sc, ax):
    blk, n = up.shape

    def body(top, bottom, rtop, rbottom, x, up, down, sc, axh, axl, xn, u, xh, xl):
        step, h = sc[0], sc[1]
        lo, hi = slice(0, blk), slice(blk, 2 * blk)
        parts = ((up[...], top, rtop, lo), (x[lo, :], top, rtop, hi))
        parts += ((x[hi, :], bottom, rbottom, lo), (down[...], bottom, rbottom, hi))
        for t, (v, a, b, s) in enumerate(parts):
            new = soft(v - step * (a[s, :] + b[s, :]), h)
            if t in (1, 2):
                xn[(t - 1) * blk : t * blk, :] = new
            d = slice(t * blk, (t + 1) * blk)
            xh[d, :], xl[d, :] = split(new)
        left((axh, axl), (xh, xl), u)

    scratch = [pltpu.VMEM((4 * blk, n), bf16)] * 2
    ins = (top, bottom, rtop, rbottom, x, up, down, sc, *ax)
    return call(body, ins, [(x.shape, f32)] * 2, 36 * blk * blk * n, scratch)


def update(mid, rup, rdown, x, sc):
    blk, n = rup.shape

    def body(mid, rup, rdown, x, sc, o):
        step, h = sc[0], sc[1]
        lo, hi = slice(0, blk), slice(blk, 2 * blk)
        for s, r in ((lo, rup), (hi, rdown)):
            o[s, :] = soft(x[s, :] - step * (mid[s, :] + r[...]), h)

    return call(body, (mid, rup, rdown, x, sc), [(x.shape, f32)], 1 << 20)[0]


def per_device(x, observed, fx, bx, fy, by, step_size, threshold):
    blk = fx.shape[2]
    rows, cols = lax.axis_size("row"), lax.axis_size("col")
    downward = [(i, i + 1) for i in range(rows - 1)]
    upward = [(i + 1, i) for i in range(rows - 1)]
    pairs = []
    for first in (0, 1):
        forth = [(i, i + 1) for i in range(first, cols - 1, 2)]
        pairs.append(forth + [(j, i) for i, j in forth])

    def row_swap(to_up, to_down):
        from_up = lax.ppermute(to_down, "row", downward)
        from_down = lax.ppermute(to_up, "row", upward)
        return from_up, from_down

    def chip_swap(a):
        return lax.ppermute(a, "col", pairs[0])

    def col_swap(b):
        return lax.ppermute(b, "col", pairs[1])

    half = cols // 2
    first_hop = [p for p in pairs[1] if set(p) != {half - 1, half}] + [(half - 1, 0), (half, cols - 1)]
    second_hop = [(0, half), (cols - 1, half - 1)]

    def columns(u, fb, merged):
        ua = chip_swap(u)
        ub = col_swap(u)
        if merged:
            w, v = near_misfit(u, ua, observed, byt, fb, blk + 120)
        else:
            pad = jnp.zeros((16, blk), f32)
            w, v = near_misfit(u, ua, observed, byt, pad, blk + 8)
        vb = lax.ppermute(v, "col", first_hop)
        wb = col_swap(w)
        relayed = lax.ppermute(vb, "col", second_hop)
        qa, qa2, q = full_misfit(w, v, ub, byt, byf)
        ra, ra2 = chip_swap(qa), chip_swap(qa2)
        return back(q, ra, ra2, wb, vb, relayed, u, fb, atx, pos, merged)

    pos = jnp.stack([lax.axis_index("row"), rows, lax.axis_index("col"), cols]).astype(jnp.int32)
    sc = jnp.concatenate([step_size, threshold])
    up, down = row_swap(x[:blk], x[blk:])
    ax, atx, byf, byt, fb = prepare(fx, bx, fy, by, pos)
    u = apply_left(x, up, down, ax)
    top, bottom, *fb = columns(u, fb, True)
    rtop, rbottom = row_swap(top, bottom)
    x, u = update_left(top, bottom, rtop, rbottom, x, up, down, sc, ax)
    top, mid, bottom = columns(u, fb, False)
    rup, rdown = row_swap(top, bottom)
    return update(mid, rup, rdown, x, sc)


def solution(mesh):
    in_specs = (
        P("row", "col"),
        P("row", "col"),
        P("row", None, None, None),
        P("row", None),
        P("col", None, None, None),
        P("col", None),
        P(),
        P(),
    )
    return jax.shard_map(
        per_device, mesh=mesh, in_specs=in_specs, out_specs=P("row", "col"), check_vma=False
    )
```

```python
import jax
import jax.numpy as jnp
from jax import lax
from jax.experimental import pallas as pl
from jax.experimental.pallas import tpu as pltpu
from jax.sharding import PartitionSpec as P

f32 = jnp.float32
bf16 = jnp.bfloat16
VMEM = pl.BlockSpec(memory_space=pltpu.VMEM)
SMEM = pl.BlockSpec(memory_space=pltpu.SMEM)
CHUNK = 256


def split(x):
    hi = x.astype(bf16)
    return hi, (x - hi.astype(f32)).astype(bf16)


def dot3(xh, xl, yh, yl):
    mm = lambda a, b: jnp.dot(a, b, preferred_element_type=f32)
    return mm(xh, yh) + (mm(xh, yl) + mm(xl, yh))


def soft(v, h):
    return v - jnp.minimum(jnp.maximum(v, -h), h)


def call(body, ins, outs, flops, scratch=(), limit=24 << 20):
    size = lambda a: a.size * a.dtype.itemsize
    return pl.pallas_call(
        body,
        out_shape=[jax.ShapeDtypeStruct(s, d) for s, d in outs],
        in_specs=[SMEM if a.size < 64 else VMEM for a in ins],
        out_specs=[VMEM for _ in outs],
        scratch_shapes=list(scratch),
        compiler_params=pltpu.CompilerParams(vmem_limit_bytes=limit),
        cost_estimate=pl.CostEstimate(
            flops=flops, bytes_accessed=sum(size(a) for a in ins), transcendentals=0
        ),
    )(*ins)


def prepare(fx, bx, fy, by, pos):
    blk = fx.shape[2]

    def body(fx, bx, fy, by, pos, axh, axl, atxh, atxl, byh, byl, byth, bytl, fb):
        row, rows, col, cols = pos[0], pos[1], pos[2], pos[3]

        def put(v, k, plain, trans):
            s = slice(k * blk, (k + 1) * blk)
            plain[0][:, s], plain[1][:, s] = split(v)
            trans[0][s, :], trans[1][s, :] = split(v.T)

        for r in range(2):
            for s in range(3):
                m = bx[r, s].astype(f32)
                if (r, s) == (0, 0):
                    m = jnp.where(row == 0, 0.0, m)
                if (r, s) == (1, 2):
                    m = jnp.where(row == rows - 1, 0.0, m)
                put(fx[r, s] * m, s, (axh.at[r], axl.at[r]), (atxh.at[r], atxl.at[r]))
        first = jnp.where(col % 2 == 0, 2, 0)
        for k, s in enumerate((first, 1, 2 - first)):
            m = by[0, s].astype(f32)
            m = jnp.where((s == 0) & (col == 0), 0.0, m)
            m = jnp.where((s == 2) & (col == cols - 1), 0.0, m)
            v = fy[0, s] * m
            put(v, k, (byh, byl), (byth, bytl))
        fb[...] = v

    outs = [((2, blk, 3 * blk), bf16)] * 2 + [((2, 3 * blk, blk), bf16)] * 2
    outs += [((blk, 3 * blk), bf16)] * 2 + [((3 * blk, blk), bf16)] * 2
    outs += [((blk, blk), f32)]
    o = call(body, (fx, bx, fy, by, pos), outs, 1 << 24)
    return o[0:2], o[2:4], o[4:6], o[6:8], o[8]


def left(ax, xs, u):
    blk = xs[0].shape[0] // 4
    for r in range(2):
        s = slice(r * blk, (r + 3) * blk)
        u[r * blk : (r + 1) * blk, :] = dot3(ax[0][r], ax[1][r], xs[0][s, :], xs[1][s, :])


def apply_left(x, up, down, ax):
    blk, n = up.shape

    def body(x, up, down, axh, axl, u, xh, xl):
        for t, v in enumerate((up[...], x[:blk, :], x[blk:, :], down[...])):
            s = slice(t * blk, (t + 1) * blk)
            xh[s, :], xl[s, :] = split(v)
        left((axh, axl), (xh, xl), u)

    scratch = [pltpu.VMEM((4 * blk, n), bf16)] * 2
    return call(body, (x, up, down, *ax), [(x.shape, f32)], 36 * blk * blk * n, scratch)[0]


def rows_of(first, second, r):
    cut, (a, b) = first.shape[0], r
    parts = []
    if a < cut:
        parts.append(first[a : min(b, cut), :])
    if b > cut:
        parts.append(second[max(a - cut, 0) : b - cut, :])
    return parts[0] if len(parts) == 1 else jnp.concatenate(parts, axis=0)


def near_misfit(u, ua, observed, byt, below, cut):
    m, blk = u.shape
    extra = below.shape[0]

    def body(u, ua, obs, byth, bytl, below, w, v):
        v[m - cut :, :] = below[...]
        for i in range(0, m, CHUNK):
            r = slice(i, i + CHUNK)
            acc = -obs[r, :]
            for k, x in enumerate((ua, u)):
                s = slice(k * blk, (k + 1) * blk)
                acc = acc + dot3(*split(x[r, :]), byth[s, :], bytl[s, :])
            here = min(max(cut - i, 0), CHUNK)
            if here:
                w[i : i + here, :] = acc[:here]
            if here < CHUNK:
                v[i + here - cut : i + CHUNK - cut, :] = acc[here:]

    outs = [((cut, blk), f32), ((m - cut + extra, blk), f32)]
    return call(body, (u, ua, observed, *byt, below), outs, 24 * m * blk * blk)


def full_misfit(w, v, ub, byt, by):
    m, blk = ub.shape

    def body(w, v, ub, byth, bytl, byh, byl, qa, qa2, q):
        b = slice(2 * blk, 3 * blk)
        for i, qa in ((0, qa), (m // 2, qa2)):
            r = slice(i, i + m // 2)
            acc = rows_of(w, v, (i, i + m // 2)) + dot3(*split(ub[r, :]), byth[b, :], bytl[b, :])
            mh, ml = split(acc)
            qa[...] = dot3(mh, ml, byh[:, :blk], byl[:, :blk])
            q[r, :] = dot3(mh, ml, byh[:, blk : 2 * blk], byl[:, blk : 2 * blk])

    outs = [((m // 2, blk), f32)] * 2 + [((m, blk), f32)]
    return call(body, (w, v, ub, *byt, *by), outs, 36 * m * blk * blk)


def back(q, ra, ra2, wb, vb, relayed, u, fb, atx, pos, merged):
    m, n = q.shape
    blk = m // 2
    cut = wb.shape[0]
    ins = (q, ra, ra2, wb, vb, relayed, u, *(() if merged else fb), *atx, pos)

    def body(q, ra, ra2, wb, vb, relayed, u, *rest):
        if merged:
            ah, al, pos, *outs = rest
        else:
            gh, gl, th, tl, ah, al, pos, *outs = rest
        half = pos[3] // 2
        special = (pos[2] == half - 1) | (pos[2] == half) | (pos[2] == 0) | (pos[2] == pos[3] - 1)
        tail = jnp.where(special, relayed[...], vb[...])
        if merged:
            *outs, gh, gl, th, tl = outs
            g = tail[m - cut : m - cut + blk]
            gh[...], gl[...] = split(g)
            th[...], tl[...] = split(g.T)
        block, flipped = (gh[...], gl[...]), (th[...], tl[...])
        p = []
        for r, a in ((0, ra), (1, ra2)):
            s = slice(r * blk, (r + 1) * blk)
            other = rows_of(wb, tail, (r * blk, (r + 1) * blk)) + dot3(*split(u[s, :]), *flipped)
            v = q[s, :] + a[...] + dot3(*split(other), *block)
            p.append(dot3(ah[r], al[r], *split(v)))
        p0 = p[0][:blk]
        p1 = p[0][blk : 2 * blk] + p[1][:blk]
        p2 = p[0][2 * blk :] + p[1][blk : 2 * blk]
        p3 = p[1][2 * blk :]
        if merged:
            top, bottom = outs
            top[:blk, :], top[blk:, :] = p0, p1
            bottom[:blk, :], bottom[blk:, :] = p2, p3
        else:
            top, mid, bottom = outs
            top[:blk, :], bottom[...] = p0, p3
            top[blk:, :] = jnp.zeros((8, n), f32)
            mid[:blk, :], mid[blk:, :] = p1, p2

    if merged:
        outs = [((m, n), f32)] * 2 + [((n, n), bf16)] * 4
    else:
        outs = [((blk + 8, n), f32), ((m, n), f32), ((blk, n), f32)]
    return call(body, ins, outs, 60 * blk * blk * n)


def update_left(top, bottom, rtop, rbottom, x, up, down, sc, ax):
    blk, n = up.shape

    def body(top, bottom, rtop, rbottom, x, up, down, sc, axh, axl, xn, u, xh, xl):
        step, h = sc[0], sc[1]
        lo, hi = slice(0, blk), slice(blk, 2 * blk)
        parts = ((up[...], top, rtop, lo), (x[lo, :], top, rtop, hi))
        parts += ((x[hi, :], bottom, rbottom, lo), (down[...], bottom, rbottom, hi))
        for t, (v, a, b, s) in enumerate(parts):
            new = soft(v - step * (a[s, :] + b[s, :]), h)
            if t in (1, 2):
                xn[(t - 1) * blk : t * blk, :] = new
            d = slice(t * blk, (t + 1) * blk)
            xh[d, :], xl[d, :] = split(new)
        left((axh, axl), (xh, xl), u)

    scratch = [pltpu.VMEM((4 * blk, n), bf16)] * 2
    ins = (top, bottom, rtop, rbottom, x, up, down, sc, *ax)
    return call(body, ins, [(x.shape, f32)] * 2, 36 * blk * blk * n, scratch)


def update(mid, rup, rdown, x, sc):
    blk, n = rup.shape

    def body(mid, rup, rdown, x, sc, o):
        step, h = sc[0], sc[1]
        lo, hi = slice(0, blk), slice(blk, 2 * blk)
        for s, r in ((lo, rup), (hi, rdown)):
            o[s, :] = soft(x[s, :] - step * (mid[s, :] + r[:blk, :]), h)

    return call(body, (mid, rup, rdown, x, sc), [(x.shape, f32)], 1 << 20)[0]


def per_device(x, observed, fx, bx, fy, by, step_size, threshold):
    blk = fx.shape[2]
    rows, cols = lax.axis_size("row"), lax.axis_size("col")
    downward = [(i, i + 1) for i in range(rows - 1)]
    upward = [(i + 1, i) for i in range(rows - 1)]
    pairs = []
    for first in (0, 1):
        forth = [(i, i + 1) for i in range(first, cols - 1, 2)]
        pairs.append(forth + [(j, i) for i, j in forth])

    def row_swap(to_up, to_down):
        from_up = lax.ppermute(to_down, "row", downward)
        from_down = lax.ppermute(to_up, "row", upward)
        return from_up, from_down

    def chip_swap(a):
        return lax.ppermute(a, "col", pairs[0])

    def col_swap(b):
        return lax.ppermute(b, "col", pairs[1])

    half = cols // 2
    first_hop = [p for p in pairs[1] if set(p) != {half - 1, half}] + [(half - 1, 0), (half, cols - 1)]
    second_hop = [(0, half), (cols - 1, half - 1)]

    def columns(u, fb, merged):
        ua = chip_swap(u)
        ub = col_swap(u)
        if merged:
            w, v = near_misfit(u, ua, observed, byt, fb, blk + 120)
        else:
            pad = jnp.zeros((16, blk), f32)
            w, v = near_misfit(u, ua, observed, byt, pad, blk + 8)
        vb = lax.ppermute(v, "col", first_hop)
        wb = col_swap(w)
        relayed = lax.ppermute(vb, "col", second_hop)
        qa, qa2, q = full_misfit(w, v, ub, byt, byf)
        ra, ra2 = chip_swap(qa), chip_swap(qa2)
        return back(q, ra, ra2, wb, vb, relayed, u, fb, atx, pos, merged)

    pos = jnp.stack([lax.axis_index("row"), rows, lax.axis_index("col"), cols]).astype(jnp.int32)
    sc = jnp.concatenate([step_size, threshold])
    up, down = row_swap(x[:blk], x[blk:])
    ax, atx, byf, byt, fb = prepare(fx, bx, fy, by, pos)
    u = apply_left(x, up, down, ax)
    top, bottom, *fb = columns(u, fb, True)
    rtop, rbottom = row_swap(top, bottom)
    x, u = update_left(top, bottom, rtop, rbottom, x, up, down, sc, ax)
    top, mid, bottom = columns(u, fb, False)
    rup, rdown = row_swap(top, bottom)
    return update(mid, rup, rdown, x, sc)


def solution(mesh):
    in_specs = (
        P("row", "col"),
        P("row", "col"),
        P("row", None, None, None),
        P("row", None),
        P("col", None, None, None),
        P("col", None),
        P(),
        P(),
    )
    return jax.shard_map(
        per_device, mesh=mesh, in_specs=in_specs, out_specs=P("row", "col"), check_vma=False
    )
```

```python
import jax
import jax.numpy as jnp
from jax import lax
from jax.experimental import pallas as pl
from jax.experimental.pallas import tpu as pltpu
from jax.sharding import PartitionSpec as P

f32 = jnp.float32
bf16 = jnp.bfloat16
VMEM = pl.BlockSpec(memory_space=pltpu.VMEM)
SMEM = pl.BlockSpec(memory_space=pltpu.SMEM)
CHUNK = 256


def split(x):
    hi = x.astype(bf16)
    return hi, (x - hi.astype(f32)).astype(bf16)


def dot3(xh, xl, yh, yl):
    mm = lambda a, b: jnp.dot(a, b, preferred_element_type=f32)
    return mm(xh, yh) + (mm(xh, yl) + mm(xl, yh))


def soft(v, h):
    return v - jnp.minimum(jnp.maximum(v, -h), h)


def call(body, ins, outs, flops, scratch=(), limit=24 << 20):
    size = lambda a: a.size * a.dtype.itemsize
    return pl.pallas_call(
        body,
        out_shape=[jax.ShapeDtypeStruct(s, d) for s, d in outs],
        in_specs=[SMEM if a.size < 64 else VMEM for a in ins],
        out_specs=[VMEM for _ in outs],
        scratch_shapes=list(scratch),
        compiler_params=pltpu.CompilerParams(vmem_limit_bytes=limit),
        cost_estimate=pl.CostEstimate(
            flops=flops, bytes_accessed=sum(size(a) for a in ins), transcendentals=0
        ),
    )(*ins)


def prepare(fx, bx, fy, by, pos):
    blk = fx.shape[2]

    def body(fx, bx, fy, by, pos, axh, axl, atxh, atxl, byh, byl, byth, bytl, fb):
        row, rows, col, cols = pos[0], pos[1], pos[2], pos[3]

        def put(v, k, plain, trans):
            s = slice(k * blk, (k + 1) * blk)
            plain[0][:, s], plain[1][:, s] = split(v)
            trans[0][s, :], trans[1][s, :] = split(v.T)

        for r in range(2):
            for s in range(3):
                m = bx[r, s].astype(f32)
                if (r, s) == (0, 0):
                    m = jnp.where(row == 0, 0.0, m)
                if (r, s) == (1, 2):
                    m = jnp.where(row == rows - 1, 0.0, m)
                put(fx[r, s] * m, s, (axh.at[r], axl.at[r]), (atxh.at[r], atxl.at[r]))
        first = jnp.where(col % 2 == 0, 2, 0)
        for k, s in enumerate((first, 1, 2 - first)):
            m = by[0, s].astype(f32)
            m = jnp.where((s == 0) & (col == 0), 0.0, m)
            m = jnp.where((s == 2) & (col == cols - 1), 0.0, m)
            v = fy[0, s] * m
            put(v, k, (byh, byl), (byth, bytl))
        fb[...] = v

    outs = [((2, blk, 3 * blk), bf16)] * 2 + [((2, 3 * blk, blk), bf16)] * 2
    outs += [((blk, 3 * blk), bf16)] * 2 + [((3 * blk, blk), bf16)] * 2
    outs += [((blk, blk), f32)]
    o = call(body, (fx, bx, fy, by, pos), outs, 1 << 24)
    return o[0:2], o[2:4], o[4:6], o[6:8], o[8]


def left(ax, xs, u):
    blk = xs[0].shape[0] // 4
    for r in range(2):
        s = slice(r * blk, (r + 3) * blk)
        u[r * blk : (r + 1) * blk, :] = dot3(ax[0][r], ax[1][r], xs[0][s, :], xs[1][s, :])


def apply_left(x, up, down, ax):
    blk, n = up.shape

    def body(x, up, down, axh, axl, u, xh, xl):
        for t, v in enumerate((up[...], x[:blk, :], x[blk:, :], down[:blk, :])):
            s = slice(t * blk, (t + 1) * blk)
            xh[s, :], xl[s, :] = split(v)
        left((axh, axl), (xh, xl), u)

    scratch = [pltpu.VMEM((4 * blk, n), bf16)] * 2
    return call(body, (x, up, down, *ax), [(x.shape, f32)], 36 * blk * blk * n, scratch)[0]


def rows_of(first, second, r):
    cut, (a, b) = first.shape[0], r
    parts = []
    if a < cut:
        parts.append(first[a : min(b, cut), :])
    if b > cut:
        parts.append(second[max(a - cut, 0) : b - cut, :])
    return parts[0] if len(parts) == 1 else jnp.concatenate(parts, axis=0)


def near_misfit(u, ua, observed, byt, below, cut):
    m, blk = u.shape
    extra = below.shape[0]

    def body(u, ua, obs, byth, bytl, below, w, v):
        v[m - cut :, :] = below[...]
        for i in range(0, m, CHUNK):
            r = slice(i, i + CHUNK)
            acc = -obs[r, :]
            for k, x in enumerate((ua, u)):
                s = slice(k * blk, (k + 1) * blk)
                acc = acc + dot3(*split(x[r, :]), byth[s, :], bytl[s, :])
            here = min(max(cut - i, 0), CHUNK)
            if here:
                w[i : i + here, :] = acc[:here]
            if here < CHUNK:
                v[i + here - cut : i + CHUNK - cut, :] = acc[here:]

    outs = [((cut, blk), f32), ((m - cut + extra, blk), f32)]
    return call(body, (u, ua, observed, *byt, below), outs, 24 * m * blk * blk)


def full_misfit(w, v, ub, byt, by):
    m, blk = ub.shape

    def body(w, v, ub, byth, bytl, byh, byl, qa, qa2, q):
        b = slice(2 * blk, 3 * blk)
        for i, qa in ((0, qa), (m // 2, qa2)):
            r = slice(i, i + m // 2)
            acc = rows_of(w, v, (i, i + m // 2)) + dot3(*split(ub[r, :]), byth[b, :], bytl[b, :])
            mh, ml = split(acc)
            qa[...] = dot3(mh, ml, byh[:, :blk], byl[:, :blk])
            q[r, :] = dot3(mh, ml, byh[:, blk : 2 * blk], byl[:, blk : 2 * blk])

    outs = [((m // 2, blk), f32)] * 2 + [((m, blk), f32)]
    return call(body, (w, v, ub, *byt, *by), outs, 36 * m * blk * blk)


def back(q, ra, ra2, wb, vb, relayed, u, fb, atx, pos, merged):
    m, n = q.shape
    blk = m // 2
    cut = wb.shape[0]
    ins = (q, ra, ra2, wb, vb, relayed, u, *(() if merged else fb), *atx, pos)

    def body(q, ra, ra2, wb, vb, relayed, u, *rest):
        if merged:
            ah, al, pos, *outs = rest
        else:
            gh, gl, th, tl, ah, al, pos, *outs = rest
        half = pos[3] // 2
        special = (pos[2] == half - 1) | (pos[2] == half) | (pos[2] == 0) | (pos[2] == pos[3] - 1)
        tail = jnp.where(special, relayed[...], vb[...])
        if merged:
            *outs, gh, gl, th, tl = outs
            g = tail[m - cut : m - cut + blk]
            gh[...], gl[...] = split(g)
            th[...], tl[...] = split(g.T)
        block, flipped = (gh[...], gl[...]), (th[...], tl[...])
        p = []
        for r, a in ((0, ra), (1, ra2)):
            s = slice(r * blk, (r + 1) * blk)
            other = rows_of(wb, tail, (r * blk, (r + 1) * blk)) + dot3(*split(u[s, :]), *flipped)
            v = q[s, :] + a[...] + dot3(*split(other), *block)
            p.append(dot3(ah[r], al[r], *split(v)))
        p0 = p[0][:blk]
        p1 = p[0][blk : 2 * blk] + p[1][:blk]
        p2 = p[0][2 * blk :] + p[1][blk : 2 * blk]
        p3 = p[1][2 * blk :]
        if merged:
            top, bottom = outs
            top[:blk, :], top[blk:, :] = p0, p1
            bottom[:blk, :], bottom[blk:, :] = p2, p3
        else:
            top, mid, bottom = outs
            top[:blk, :], bottom[...] = p0, p3
            top[blk:, :] = jnp.zeros((8, n), f32)
            mid[:blk, :], mid[blk:, :] = p1, p2

    if merged:
        outs = [((m, n), f32)] * 2 + [((n, n), bf16)] * 4
    else:
        outs = [((blk + 8, n), f32), ((m, n), f32), ((blk, n), f32)]
    return call(body, ins, outs, 60 * blk * blk * n)


def update_left(top, bottom, rtop, rbottom, x, up, down, sc, ax):
    blk, n = up.shape

    def body(top, bottom, rtop, rbottom, x, up, down, sc, axh, axl, xn, u, xh, xl):
        step, h = sc[0], sc[1]
        lo, hi = slice(0, blk), slice(blk, 2 * blk)
        parts = ((up[...], top, rtop, lo), (x[lo, :], top, rtop, hi))
        parts += ((x[hi, :], bottom, rbottom, lo), (down[:blk, :], bottom, rbottom, hi))
        for t, (v, a, b, s) in enumerate(parts):
            new = soft(v - step * (a[s, :] + b[s, :]), h)
            if t in (1, 2):
                xn[(t - 1) * blk : t * blk, :] = new
            d = slice(t * blk, (t + 1) * blk)
            xh[d, :], xl[d, :] = split(new)
        left((axh, axl), (xh, xl), u)

    scratch = [pltpu.VMEM((4 * blk, n), bf16)] * 2
    ins = (top, bottom, rtop, rbottom, x, up, down, sc, *ax)
    return call(body, ins, [(x.shape, f32)] * 2, 36 * blk * blk * n, scratch)


def update(mid, rup, rdown, x, sc):
    blk, n = rup.shape

    def body(mid, rup, rdown, x, sc, o):
        step, h = sc[0], sc[1]
        lo, hi = slice(0, blk), slice(blk, 2 * blk)
        for s, r in ((lo, rup), (hi, rdown)):
            o[s, :] = soft(x[s, :] - step * (mid[s, :] + r[:blk, :]), h)

    return call(body, (mid, rup, rdown, x, sc), [(x.shape, f32)], 1 << 20)[0]


def per_device(x, observed, fx, bx, fy, by, step_size, threshold):
    blk = fx.shape[2]
    rows, cols = lax.axis_size("row"), lax.axis_size("col")
    downward = [(i, i + 1) for i in range(rows - 1)]
    upward = [(i + 1, i) for i in range(rows - 1)]
    pairs = []
    for first in (0, 1):
        forth = [(i, i + 1) for i in range(first, cols - 1, 2)]
        pairs.append(forth + [(j, i) for i, j in forth])

    def row_swap(to_up, to_down):
        from_up = lax.ppermute(to_down, "row", downward)
        from_down = lax.ppermute(to_up, "row", upward)
        return from_up, from_down

    def chip_swap(a):
        return lax.ppermute(a, "col", pairs[0])

    def col_swap(b):
        return lax.ppermute(b, "col", pairs[1])

    half = cols // 2
    first_hop = [p for p in pairs[1] if set(p) != {half - 1, half}] + [(half - 1, 0), (half, cols - 1)]
    second_hop = [(0, half), (cols - 1, half - 1)]

    def columns(u, fb, merged):
        ua = chip_swap(u)
        ub = col_swap(u)
        if merged:
            w, v = near_misfit(u, ua, observed, byt, fb, blk + 120)
        else:
            pad = jnp.zeros((16, blk), f32)
            w, v = near_misfit(u, ua, observed, byt, pad, blk + 8)
        vb = lax.ppermute(v, "col", first_hop)
        wb = col_swap(w)
        relayed = lax.ppermute(vb, "col", second_hop)
        qa, qa2, q = full_misfit(w, v, ub, byt, byf)
        ra, ra2 = chip_swap(qa), chip_swap(qa2)
        return back(q, ra, ra2, wb, vb, relayed, u, fb, atx, pos, merged)

    pos = jnp.stack([lax.axis_index("row"), rows, lax.axis_index("col"), cols]).astype(jnp.int32)
    sc = jnp.concatenate([step_size, threshold])
    up, down = row_swap(x[: blk + 8], x[blk:])
    ax, atx, byf, byt, fb = prepare(fx, bx, fy, by, pos)
    u = apply_left(x, up, down, ax)
    top, bottom, *fb = columns(u, fb, True)
    rtop, rbottom = row_swap(top, bottom)
    x, u = update_left(top, bottom, rtop, rbottom, x, up, down, sc, ax)
    top, mid, bottom = columns(u, fb, False)
    rup, rdown = row_swap(top, bottom)
    return update(mid, rup, rdown, x, sc)


def solution(mesh):
    in_specs = (
        P("row", "col"),
        P("row", "col"),
        P("row", None, None, None),
        P("row", None),
        P("col", None, None, None),
        P("col", None),
        P(),
        P(),
    )
    return jax.shard_map(
        per_device, mesh=mesh, in_specs=in_specs, out_specs=P("row", "col"), check_vma=False
    )
```
